32 devices in a mesh: sec: 4 (over x, core), gx: 8 (over z, y).
Axes of the slice: x: 2, y: 2, z: 4, core: 2. Of those that a mesh axis runs over, the one named last changes fastest.
Arguments:
- ocean_state: float32 [4, 4, 96, 256], P(None, None, 'gx'), may hold values from -4 to 4
- heat_first: float32 [4, 96, 256], P(None, 'gx'), may hold values from 0 to 1.5
- wind_stress: float32 [2, 96, 256], P(None, 'gx'), may hold values from -3 to 3
- shortwave: float32 [96, 256], P('gx'), may hold values from 1 to 6
- sea_mask: int32 [96, 256], P('gx'), may hold values from 0 to 1, as said below
- owner_cols: int32 [8, 3, 8, 128], P('gx'), may hold values from -1 to 3071, as said below
- tracers: float32 [19, 4, 32768], P(None, None, ('sec', 'gx')), may hold values from 0.2 to 2
Outputs:
- tracers_out: float32 [19, 4, 32768], P(None, None, ('sec', 'gx'))
- heating_out: float32 [4, 32768], P(None, ('sec', 'gx'))
The draws below stay inside these ranges and needn't reach their ends.
Inputs may be any that keep to these rules, and one draw needn't show every extreme that they name: `sea_mask`: 1 marks a sea column, 0 land; within a strip, column j is sea wherever j % 128 = 127 and in the last 128 columns. `owner_cols`: entry [g, s, h, j] is slot j of the list of strip g's sea columns owned by the tracer device of section s + 1 and gx index h, strip g being the cells at gx index g; a column is x 256 + y with x counted within the strip, and -1 marks an empty slot. Every sea column of a strip stands in exactly one slot and no land column does; the used slots of a list come first, in ascending order; every list holds at least one column. In every draw one tracer device has full lists from every strip.
All inputs are finite; a program needn't handle non-finite values.
Results may differ from the reference program's by a relative error of at most 0.00002.
Values sent between devices are 32-bit elements; how exact they have to be, the bound alone decides.
A program may use at most 192 MiB of HBM per device.

```python
import math
import jax
import jax.numpy as jnp
import numpy as np
from jax import lax

SPECIES = 19
LEVELS = 4
LAT_CELLS = 256
STEPS = 2
SUBSTEPS = 1
PAIR_SLOTS = 128
STRIP_COLS = 3072
LON_CELLS = 96
DEV_SLOTS = 1024
ALL_SLOTS = 32768
N_SEC = 4
N_GX = 8


def ocean_world(key):
    strips = N_GX
    owners = (N_SEC - 1) * N_GX
    land_share = jax.random.randint(jax.random.fold_in(key, 101), (strips, 1), 10, 90)
    dice_rolls = jax.random.randint(jax.random.fold_in(key, 102), (strips, STRIP_COLS), 0, 100)
    column_ids = jnp.broadcast_to(jnp.arange(STRIP_COLS, dtype=jnp.int32)[None, :], (strips, STRIP_COLS))
    forced = jnp.logical_or(column_ids % PAIR_SLOTS == PAIR_SLOTS - 1, column_ids >= STRIP_COLS - PAIR_SLOTS)
    sea_cells = jnp.logical_or(dice_rolls >= land_share, forced).astype(jnp.int32)
    popular = jax.random.randint(jax.random.fold_in(key, 103), (1, owners), 0, 1000)
    jitter = jax.random.randint(jax.random.fold_in(key, 104), (strips, owners), 0, 1000)
    chosen = jax.random.randint(jax.random.fold_in(key, 105), (), 0, owners)
    owner_ids = jnp.arange(owners, dtype=jnp.int32)[None, :]
    scores = (jitter + popular + 4000 * (owner_ids == chosen).astype(jnp.int32)) * owners + owner_ids
    ranking = jnp.argsort(-scores, axis=1).astype(jnp.int32)
    position = (jnp.cumsum(sea_cells, axis=1) - 1).astype(jnp.int32)
    first_layer = position < owners
    rest = jnp.maximum(position - owners, 0)
    rank_index = jnp.clip(rest // (PAIR_SLOTS - 1), 0, owners - 1)
    owner_rest = jnp.take_along_axis(ranking, rank_index, axis=1)
    owner_of = jnp.where(first_layer, jnp.clip(position, 0, owners - 1), owner_rest)
    slot_index = jnp.where(first_layer, 0, 1 + rest % (PAIR_SLOTS - 1))
    target = jnp.where(sea_cells == 1, owner_of * PAIR_SLOTS + slot_index, owners * PAIR_SLOTS)
    strip_ids = jnp.broadcast_to(jnp.arange(strips, dtype=jnp.int32)[:, None], (strips, STRIP_COLS))
    slot_lists = jnp.full((strips, owners * PAIR_SLOTS), -1, jnp.int32)
    slot_lists = slot_lists.at[strip_ids, target].set(column_ids, mode='drop')
    return (sea_cells, slot_lists.reshape(strips, N_SEC - 1, N_GX, PAIR_SLOTS))


def draw_sea_mask(key, part):
    sea_cells, slot_lists = ocean_world(key)
    return sea_cells.reshape(LON_CELLS, LAT_CELLS)


def draw_owner_cols(key, part):
    sea_cells, slot_lists = ocean_world(key)
    return slot_lists


def block_scale(key, extent, cuts, smallest, high):
    factor_of = 1.0
    for axis_at, blocks in cuts:
        draws = jax.random.uniform(jax.random.fold_in(jax.random.fold_in(key, 6), axis_at), (blocks,), jnp.float32, smallest / len(cuts), high / len(cuts))
        factor_of = factor_of * jnp.repeat(jnp.exp(draws), extent[axis_at] // blocks).reshape((-1,) + (1,) * (len(extent) - 1 - axis_at))
    return factor_of


def centred(rng, shape, deviation, reach, cuts=(), kind=jnp.bfloat16):
    level = block_scale(rng, shape, cuts, -0.22, 0.18) if cuts else 1.0
    entries = jax.random.normal(rng, shape, jnp.float32) * deviation * level
    return jnp.minimum(jnp.maximum(entries, -reach), reach).astype(kind)


def setup_inputs(seed: int = 0) -> dict:
    streams_of = jax.random.split(jax.random.key(seed), 8)
    return {
        "ocean_state": centred(streams_of[0], (4, LEVELS, LON_CELLS, LAT_CELLS), 1.0, 4.0, ((2, 8),), jnp.float32),
        "heat_first": jnp.clip(1.5 * jax.random.uniform(streams_of[1], (LEVELS, LON_CELLS, LAT_CELLS), jnp.float32) ** block_scale(streams_of[1], (LEVELS, LON_CELLS, LAT_CELLS), ((1, 8),), -0.2, 0.2), 0.0, 1.5),
        "wind_stress": centred(streams_of[2], (2, LON_CELLS, LAT_CELLS), 0.6, 3.0, ((1, 8),), jnp.float32),
        "shortwave": jnp.clip(jnp.exp(math.log(6.0) - 1.7917595 * jax.random.uniform(streams_of[3], (LON_CELLS, LAT_CELLS), jnp.float32) ** block_scale(streams_of[3], (LON_CELLS, LAT_CELLS), ((0, 8),), -0.2, 0.2)), 1.0, 6.0),
        "sea_mask": draw_sea_mask(jax.random.fold_in(streams_of[7], 71), 0),
        "owner_cols": draw_owner_cols(jax.random.fold_in(streams_of[7], 71), 0),
        "tracers": jnp.clip(0.2 + 1.8 * jax.random.uniform(streams_of[6], (SPECIES, LEVELS, ALL_SLOTS), jnp.float32) ** block_scale(streams_of[6], (SPECIES, LEVELS, ALL_SLOTS), ((2, 32),), -0.2, 0.2), 0.2, 2.0),
    }


DT_OCEAN = 0.15
VISCOSITY = 0.2
DIFFUSIVITY = 0.15
DAMPING = 0.05
CORIOLIS = 0.8
HEAT_GAIN = 4.0
ONE_THIRD = 1.0 / 3.0
TWO_THIRDS = 2.0 / 3.0
DT_BIO = 0.8
W_LIMIT = 0.35
W_GAIN = 0.25
KV_BASE = 0.05
KV_SHEAR = 0.3
GAS_RATE = 0.5
WATER_ATTEN = 0.15
CHLORO_ATTEN = 0.1
HEATUP_PER_STEP = 0.5
GROWTH = 0.6
GRAZING = 0.4
REMINERAL = 0.2
EXCRETION = 0.1
PHYTO_LOSS = 0.05
ZOO_LOSS = 0.05
ASSIMILATE = 0.6
YIELDS = np.array([0.0, 0.0, 0.0, 0.0, -1.3, 1.0, 0.16, 0.9, -0.6, 0.4, 1.2, -0.8, 0.5, 0.3, -0.4, 0.7, -1.0, 0.2, 0.6], np.float32)
DECAYS = np.array([0.0, 0.0, 0.0, 0.0, 0.02, 0.01, 0.05, 0.03, 0.08, 0.04, 0.02, 0.06, 0.1, 0.03, 0.07, 0.05, 0.02, 0.09, 0.04], np.float32)
GAS_ON = np.array([0, 0, 0, 0, 1, 1] + [0] * 13, np.float32)
SOLUBILITY_BASE = np.array([0, 0, 0, 0, 1.2, 1.0] + [0] * 13, np.float32)
SOLUBILITY_HEAT = np.array([0, 0, 0, 0, -0.5, -0.3] + [0] * 13, np.float32)
SOLUBILITY_BRINE = np.array([0, 0, 0, 0, 0.1, 0.3] + [0] * 13, np.float32)


def coriolis_profile(count):
    lat_index = jnp.arange(count, dtype=jnp.float32)
    return CORIOLIS * (2.0 * (lat_index + 0.5) / count - 1.0)


def ocean_tendency(padded, heating, sea_cells, stress, coriolis_y):
    centre = padded[:, :, 1:-1]
    east_cells = padded[:, :, 2:]
    west_cells = padded[:, :, :-2]
    edge_zeros = jnp.zeros_like(centre[..., :1])
    north_cells = jnp.concatenate([centre[..., 1:], edge_zeros], axis=-1)
    south_cells = jnp.concatenate([edge_zeros, centre[..., :-1]], axis=-1)
    laplace = east_cells + west_cells + north_cells + south_cells - 4.0 * centre
    along_x = 0.5 * (east_cells - west_cells)
    along_y = 0.5 * (north_cells - south_cells)
    zonal_vel = centre[0]
    meridional = centre[1]
    levels = centre.shape[1]
    top_level = (jnp.arange(levels) == 0).astype(jnp.float32)[:, None, None]
    zonal_rate = coriolis_y * meridional - DAMPING * zonal_vel + VISCOSITY * laplace[0] + top_level * stress[0]
    merid_rate = -coriolis_y * zonal_vel - DAMPING * meridional + VISCOSITY * laplace[1] + top_level * stress[1]
    heat_rate = -(zonal_vel * along_x[2] + meridional * along_y[2]) + DIFFUSIVITY * laplace[2] + HEAT_GAIN * heating
    salt_rate = -(zonal_vel * along_x[3] + meridional * along_y[3]) + DIFFUSIVITY * laplace[3]
    return jnp.stack([zonal_rate, merid_rate, heat_rate, salt_rate]) * sea_cells


def wrap_lon(field):
    return jnp.concatenate([field[..., -1:, :], field, field[..., :1, :]], axis=-2)


def runge_step(current, heating, sea_cells, stress, coriolis_y):
    segment_one = current + DT_OCEAN * ocean_tendency(wrap_lon(current), heating, sea_cells, stress, coriolis_y)
    segment_two = 0.75 * current + 0.25 * (segment_one + DT_OCEAN * ocean_tendency(wrap_lon(segment_one), heating, sea_cells, stress, coriolis_y))
    return ONE_THIRD * current + TWO_THIRDS * (segment_two + DT_OCEAN * ocean_tendency(wrap_lon(segment_two), heating, sea_cells, stress, coriolis_y))


def column_fields(current, zonal_padded, stress, shortwave):
    zonal_vel = current[0]
    meridional = current[1]
    levels = current.shape[1]
    edge_zeros = jnp.zeros_like(meridional[..., :1])
    merid_north = jnp.concatenate([meridional[..., 1:], edge_zeros], axis=-1)
    merid_south = jnp.concatenate([edge_zeros, meridional[..., :-1]], axis=-1)
    divergence = 0.5 * (zonal_padded[:, 2:] - zonal_padded[:, :-2]) + 0.5 * (merid_north - merid_south)
    from_bottom = jnp.cumsum(divergence[::-1], axis=0)[::-1]
    below_top = (jnp.arange(levels) > 0).astype(jnp.float32)[:, None, None]
    upwelling = W_LIMIT * jnp.tanh(W_GAIN * from_bottom) * below_top
    shear_sq = (zonal_vel[1:] - zonal_vel[:-1]) ** 2 + (meridional[1:] - meridional[:-1]) ** 2
    mixing = KV_BASE + KV_SHEAR * shear_sq / (1.0 + shear_sq)
    mixing = jnp.concatenate([jnp.zeros_like(mixing[:1]), mixing], axis=0)
    grid_box_space = jnp.stack([current[2], current[3], upwelling, mixing])
    surface = jnp.stack([stress[0] * stress[0] + stress[1] * stress[1], shortwave])
    return grid_box_space.reshape(4, levels, -1), surface.reshape(2, -1)


def minmod(one_side, other_side):
    return jnp.maximum(0.0, jnp.minimum(one_side, other_side)) + jnp.minimum(0.0, jnp.maximum(one_side, other_side))


def biogeochem(grid_box_space, surface, validity, species_now):
    marine_thermal_state = grid_box_space[0]
    brine_content = grid_box_space[1]
    upwelling = grid_box_space[2]
    mixing = grid_box_space[3]
    wind_power = surface[0]
    sunlight = surface[1]
    level_zero = jnp.zeros_like(species_now[:, :1])
    step_diff = species_now[:, 1:] - species_now[:, :-1]
    slopes = minmod(jnp.concatenate([step_diff, level_zero], axis=1), jnp.concatenate([level_zero, step_diff], axis=1))
    courant = jnp.abs(upwelling) * DT_BIO
    above_cell = jnp.concatenate([species_now[:, :1], species_now[:, :-1]], axis=1)
    above_slope = jnp.concatenate([slopes[:, :1], slopes[:, :-1]], axis=1)
    from_below = species_now - 0.5 * (1.0 - courant) * slopes
    from_above = above_cell + 0.5 * (1.0 - courant) * above_slope
    updraft_flux = jnp.maximum(upwelling, 0.0) * from_below + jnp.minimum(upwelling, 0.0) * from_above
    advect = jnp.concatenate([updraft_flux[:, 1:], level_zero], axis=1) - updraft_flux
    down_mix = mixing * (above_cell - species_now)
    diffuse = down_mix - jnp.concatenate([down_mix[:, 1:], level_zero], axis=1)
    transported = species_now + DT_BIO * (advect + diffuse)
    transfer = GAS_RATE * wind_power / (1.0 + wind_power)
    dissolved_limit = SOLUBILITY_BASE[:, None] + SOLUBILITY_HEAT[:, None] * marine_thermal_state[0] + SOLUBILITY_BRINE[:, None] * brine_content[0]
    exchange_top = GAS_ON[:, None] * DT_BIO * transfer * (dissolved_limit - transported[:, 0])
    transported = jnp.concatenate([(transported[:, 0] + exchange_top)[:, None], transported[:, 1:]], axis=1)
    nutrient = transported[0]
    phytoplankton = transported[1]
    zooplank = transported[2]
    detritus = transported[3]
    extinction = WATER_ATTEN + CHLORO_ATTEN * jnp.abs(phytoplankton)
    above_ext = jnp.cumsum(extinction, axis=0) - extinction
    top_light = sunlight * jnp.exp(-above_ext)
    mid_light = top_light * jnp.exp(-0.5 * extinction)
    heating = top_light - top_light * jnp.exp(-extinction)
    heatup_increment = jnp.exp(HEATUP_PER_STEP * marine_thermal_state)
    growth = GROWTH * heatup_increment * mid_light / (mid_light + 1.0) * jnp.abs(nutrient) / (jnp.abs(nutrient) + 1.0) * phytoplankton
    grazing = GRAZING * heatup_increment * phytoplankton * phytoplankton / (phytoplankton * phytoplankton + 1.0) * zooplank
    remineral = REMINERAL * heatup_increment * detritus
    nutrient_rate = -growth + remineral + EXCRETION * zooplank
    phyto_rate = growth - grazing - PHYTO_LOSS * phytoplankton
    zoo_rate = ASSIMILATE * grazing - EXCRETION * zooplank - ZOO_LOSS * zooplank
    detritus_rate = (1.0 - ASSIMILATE) * grazing + PHYTO_LOSS * phytoplankton + ZOO_LOSS * zooplank - remineral
    others = YIELDS[4:, None, None] * (remineral - growth) - DECAYS[4:, None, None] * transported[4:]
    change = jnp.concatenate([jnp.stack([nutrient_rate, phyto_rate, zoo_rate, detritus_rate]), others], axis=0)
    reacted = transported + DT_BIO * change
    return validity * reacted + (1.0 - validity) * species_now, validity * heating


def by_device(slot_volume, slot_surface, validity, species_now):
    devices = N_SEC * N_GX
    volume_dev = jnp.moveaxis(slot_volume.reshape(4, LEVELS, devices, DEV_SLOTS), 2, 0)
    surface_dev = jnp.moveaxis(slot_surface.reshape(2, devices, DEV_SLOTS), 1, 0)
    valid_dev = validity.reshape(devices, DEV_SLOTS)
    species_dev = jnp.moveaxis(species_now.reshape(SPECIES, LEVELS, devices, DEV_SLOTS), 2, 0)

    def one_device(pieces):
        return biogeochem(pieces[0], pieces[1], pieces[2], pieces[3])

    new_species, heating = lax.map(one_device, (volume_dev, surface_dev, valid_dev, species_dev))
    return jnp.moveaxis(new_species, 0, 2).reshape(SPECIES, LEVELS, -1), jnp.moveaxis(heating, 0, 1).reshape(LEVELS, -1)


def reference(ocean_state, heat_first, wind_stress, shortwave, sea_mask, owner_cols, tracers):
    sea_cells = sea_mask.astype(jnp.float32)
    coriolis_y = coriolis_profile(LAT_CELLS)
    offsets = (jnp.arange(N_GX, dtype=jnp.int32) * STRIP_COLS)[:, None, None, None]
    global_cols = jnp.where(owner_cols >= 0, owner_cols + offsets, -1).astype(jnp.int32)
    ordered = jnp.transpose(global_cols, (1, 2, 0, 3)).reshape(-1)
    dead_slots = jnp.full((N_GX * N_GX * PAIR_SLOTS,), -1, jnp.int32)
    slot_table = jnp.concatenate([dead_slots, ordered]).astype(jnp.int32)
    validity = (slot_table >= 0).astype(jnp.float32)
    safe_index = jnp.maximum(slot_table, 0).astype(jnp.int32)
    current = ocean_state
    heating = heat_first
    species_now = tracers
    heat_slots = jnp.zeros((LEVELS, ALL_SLOTS), jnp.float32)
    for coupling in range(STEPS):
        for substep in range(SUBSTEPS):
            current = runge_step(current, heating, sea_cells, wind_stress, coriolis_y)
        zonal_padded = wrap_lon(current[0])
        grid_box_space, surface = column_fields(current, zonal_padded, wind_stress, shortwave)
        slot_volume = jnp.take(grid_box_space, safe_index, axis=2) * validity
        slot_surface = jnp.take(surface, safe_index, axis=1) * validity
        species_now, heat_slots = by_device(slot_volume, slot_surface, validity, species_now)
        if coupling + 1 < STEPS:
            placed = jnp.zeros((LEVELS, LON_CELLS * LAT_CELLS), jnp.float32).at[:, safe_index].add(heat_slots)
            heating = placed.reshape(LEVELS, LON_CELLS, LAT_CELLS)
    return species_now, heat_slots
```

```python
import functools

import jax
import jax.numpy as jnp
import numpy as np
from jax import lax
from jax.experimental import pallas as pl
from jax.experimental.pallas import tpu as pltpu
from jax.sharding import PartitionSpec as P

STEPS = 2


DT_OCEAN = 0.15
VISCOSITY = 0.2
DIFFUSIVITY = 0.15
DAMPING = 0.05
CORIOLIS = 0.8
HEAT_GAIN = 4.0
ONE_THIRD = 1.0 / 3.0
TWO_THIRDS = 2.0 / 3.0
DT_BIO = 0.8
W_LIMIT = 0.35
W_GAIN = 0.25
KV_BASE = 0.05
KV_SHEAR = 0.3
GAS_RATE = 0.5
WATER_ATTEN = 0.15
CHLORO_ATTEN = 0.1
HEATUP_PER_STEP = 0.5
GROWTH = 0.6
GRAZING = 0.4
REMINERAL = 0.2
EXCRETION = 0.1
PHYTO_LOSS = 0.05
ZOO_LOSS = 0.05
ASSIMILATE = 0.6
YIELDS = np.array(
    [
        0.0,
        0.0,
        0.0,
        0.0,
        -1.3,
        1.0,
        0.16,
        0.9,
        -0.6,
        0.4,
        1.2,
        -0.8,
        0.5,
        0.3,
        -0.4,
        0.7,
        -1.0,
        0.2,
        0.6,
    ],
    np.float32,
)
DECAYS = np.array(
    [
        0.0,
        0.0,
        0.0,
        0.0,
        0.02,
        0.01,
        0.05,
        0.03,
        0.08,
        0.04,
        0.02,
        0.06,
        0.1,
        0.03,
        0.07,
        0.05,
        0.02,
        0.09,
        0.04,
    ],
    np.float32,
)
GAS_ON = np.array([0, 0, 0, 0, 1, 1] + [0] * 13, np.float32)
SOLUBILITY_BASE = np.array([0, 0, 0, 0, 1.2, 1.0] + [0] * 13, np.float32)
SOLUBILITY_HEAT = np.array([0, 0, 0, 0, -0.5, -0.3] + [0] * 13, np.float32)
SOLUBILITY_BRINE = np.array([0, 0, 0, 0, 0.1, 0.3] + [0] * 13, np.float32)

MESH = pl.DeviceIdType.MESH
HALO = 8
LANES = 128
ROWS_SENT = 16


def minmod(one_side, other_side):
    return jnp.maximum(0.0, jnp.minimum(one_side, other_side)) + jnp.minimum(
        0.0, jnp.maximum(one_side, other_side)
    )


def transport_weights(upwelling):
    return [
        None
        if w is None
        else (jnp.maximum(w, 0.0), jnp.minimum(w, 0.0), 0.5 * (1.0 - DT_BIO * jnp.abs(w)))
        for w in upwelling
    ]


def transport(column, weights, mixing):
    levels = len(column)
    diffs = [column[k + 1] - column[k] for k in range(levels - 1)]
    slopes = [None] + [minmod(diffs[k], diffs[k - 1]) for k in range(1, levels - 1)] + [None]
    flux = [None] * (levels + 1)
    for k in range(1, levels):
        up, down, half = weights[k]
        from_below = column[k] if slopes[k] is None else column[k] - half * slopes[k]
        from_above = column[k - 1] if slopes[k - 1] is None else column[k - 1] + half * slopes[k - 1]
        flux[k] = up * from_below + down * from_above + mixing[k] * diffs[k - 1]
    out = []
    for k in range(levels):
        if k == 0:
            gain = flux[1]
        elif k == levels - 1:
            gain = -flux[k]
        else:
            gain = flux[k + 1] - flux[k]
        out.append(column[k] + DT_BIO * gain)
    return out


def light_profile(phyto, sunlight):
    mids, heats = [], []
    top = sunlight
    for p in phyto:
        extinction = WATER_ATTEN + CHLORO_ATTEN * jnp.abs(p)
        mid_pass = jnp.exp(-0.5 * extinction)
        mids.append(top * mid_pass)
        after = top * jnp.exp(-extinction)
        heats.append(top - after)
        top = after
    return mids, heats


def ceil_to(value, unit):
    return (value + unit - 1) // unit * unit


def whole_kernel(
    sections,
    strips,
    levels,
    width,
    lat,
    state_ref,
    heat_ref,
    wind_ref,
    sun_ref,
    sea_ref,
    lists_ref,
    phyto_ref,
    trac_ref,
    out_c,
    out_h,
    grid,
    halo_out,
    halo_in,
    phyto_in,
    placed,
    onehot,
    phyto_grid,
    rim_out,
    rim_in,
    fields,
    send,
    recv,
    halo_ssem,
    halo_rsem,
    phyto_ssem,
    phyto_rsem,
    rim_ssem,
    rim_rsem,
    field_ssem,
    field_rsem,
):
    owners = (sections - 1) * strips
    species = trac_ref.shape[0]
    padded_rows = grid.shape[1]
    sec = lax.axis_index("sec")
    strip = lax.axis_index("gx")
    right = lax.rem(strip + 1, strips)
    left = lax.rem(strip + strips - 1, strips)
    me = (sec - 1) * strips + strip
    lat_shift = lat.bit_length() - 1
    halves = lat // LANES
    place_rows = placed.shape[0] // (3 * levels)
    first_heat = 4 * levels
    first_wind = 5 * levels
    sun_row = first_wind + 2
    sea_row = first_wind + 3

    @pl.when(sec == 0)
    def _():
        out_c[...] = trac_ref[...]
        out_h[...] = jnp.zeros_like(out_h)

    @pl.when(sec > 0)
    def _():
        def channel(c, rows):
            if c < first_heat:
                return state_ref[c, rows, :]
            if c < first_wind:
                return heat_ref[c - first_heat, rows, :]
            if c < sun_row:
                return wind_ref[c - first_wind, rows, :]
            if c == sun_row:
                return sun_ref[rows, :]
            return sea_ref[rows, :].astype(jnp.float32)

        for c in range(grid.shape[0]):
            halo_out[0, c] = channel(c, slice(width - HALO, width))
            halo_out[1, c] = channel(c, slice(0, HALO))

        barrier = pltpu.get_barrier_semaphore()

        def greet(i, carry):
            t = lax.rem(me + i, owners)
            pl.semaphore_signal(
                barrier, inc=1, device_id=(1 + t // strips, lax.rem(t, strips)), device_id_type=MESH
            )
            return carry

        lax.fori_loop(1, owners, greet, 0)
        pl.semaphore_wait(barrier, owners - 1)

        def edge_copy(out_ref, in_ref, ssem, rsem, side):
            return pltpu.make_async_remote_copy(
                src_ref=out_ref.at[side],
                dst_ref=in_ref.at[side],
                send_sem=ssem.at[side],
                recv_sem=rsem.at[side],
                device_id=(sec, right if side == 0 else left),
                device_id_type=MESH,
            )

        halo_copies = [
            edge_copy(halo_out, halo_in, halo_ssem, halo_rsem, side) for side in range(2)
        ]

        def phyto_copy(t, slot):
            target = lax.rem(t, strips)
            return pltpu.make_async_remote_copy(
                src_ref=phyto_ref.at[:, pl.ds(pl.multiple_of(target * LANES, LANES), LANES)],
                dst_ref=phyto_in.at[slot],
                send_sem=phyto_ssem.at[t],
                recv_sem=phyto_rsem.at[slot],
                device_id=(1 + t // strips, target),
                device_id_type=MESH,
            )

        def send_phyto(i, carry):
            phyto_copy(lax.rem(me + i, owners), me).start()
            return carry

        lax.fori_loop(1, owners, send_phyto, 0)
        for copy in halo_copies:
            copy.start()

        phyto_in[me] = phyto_ref[:, pl.ds(pl.multiple_of(strip * LANES, LANES), LANES)]

        for c in range(grid.shape[0]):
            if padded_rows > width + 2 * HALO:
                grid[c, width + 2 * HALO :, :] = jnp.zeros(
                    (padded_rows - width - 2 * HALO, lat), jnp.float32
                )
            grid[c, HALO : HALO + width, :] = channel(c, slice(0, width))

        def wait_phyto(i, carry):
            t = lax.rem(me + i, owners)
            phyto_copy(t, t).wait()
            return carry

        lax.fori_loop(1, owners, wait_phyto, 0)

        lat_index = lax.broadcasted_iota(jnp.int32, (lat, LANES), 0)
        lon_index = lax.broadcasted_iota(jnp.int32, (place_rows, LANES), 0)

        def spread(l, carry):
            listed = lists_ref[pl.ds(l, 1), :]
            x = listed >> lat_shift
            y = listed & (lat - 1)
            lanes = pl.ds(pl.multiple_of(l * LANES, LANES), LANES)
            onehot[:, lanes] = jnp.where(lat_index == y, 1.0, 0.0).astype(jnp.bfloat16)
            here = lon_index == x
            values = phyto_in[l]
            for k in range(levels):
                rest = values[k : k + 1, :]
                for part in range(3):
                    term = rest.astype(jnp.bfloat16).astype(jnp.float32)
                    rest = rest - term
                    row = (3 * k + part) * place_rows
                    placed[row : row + place_rows, lanes] = jnp.where(here, term, 0.0).astype(
                        jnp.bfloat16
                    )
            return carry

        lax.fori_loop(0, owners, spread, 0)
        spread_out = lax.dot_general(
            placed[...],
            onehot[...],
            (((1,), (1,)), ((), ())),
            preferred_element_type=jnp.float32,
        )
        for k in range(levels):
            base = 3 * k * place_rows
            own = (
                spread_out[base : base + width]
                + spread_out[base + place_rows : base + place_rows + width]
                + spread_out[base + 2 * place_rows : base + 2 * place_rows + width]
            )
            phyto_grid[k] = jnp.zeros((padded_rows, lat), jnp.float32)
            phyto_grid[k, HALO : HALO + width, :] = own
            rim_out[0, 2 * k : 2 * k + 2, :] = own[width - 2 : width]
            rim_out[1, 2 * k : 2 * k + 2, :] = own[0:2]

        rim_copies = [edge_copy(rim_out, rim_in, rim_ssem, rim_rsem, side) for side in range(2)]
        for copy in rim_copies:
            copy.start()
        for copy in halo_copies:
            copy.wait()
        for c in range(grid.shape[0]):
            grid[c, 0:HALO, :] = halo_in[0, c]
            grid[c, HALO + width : 2 * HALO + width, :] = halo_in[1, c]

        lane = lax.broadcasted_iota(jnp.int32, (padded_rows, lat), 1)
        not_last = lane < lat - 1
        not_first = lane > 0
        coriolis_y = CORIOLIS * (2.0 * (lane.astype(jnp.float32) + 0.5) / lat - 1.0)

        def around(field):
            east = pltpu.roll(field, padded_rows - 1, 0)
            west = pltpu.roll(field, 1, 0)
            north = jnp.where(not_last, pltpu.roll(field, lat - 1, 1), 0.0)
            south = jnp.where(not_first, pltpu.roll(field, 1, 1), 0.0)
            return east, west, north, south

        def rates(u, v, q, r, heating, k):
            def flow(field):
                east, west, north, south = around(field)
                return east + west + north + south - 4.0 * field

            def carried(field):
                east, west, north, south = around(field)
                return (
                    DIFFUSIVITY * (east + west + north + south - 4.0 * field)
                    - (u * (0.5 * (east - west)) + v * (0.5 * (north - south)))
                )

            sea = grid[sea_row]
            du = coriolis_y * v - DAMPING * u + VISCOSITY * flow(u)
            dv = -coriolis_y * u - DAMPING * v + VISCOSITY * flow(v)
            if k == 0:
                du = du + grid[first_wind]
                dv = dv + grid[first_wind + 1]
            dq = carried(q) + HEAT_GAIN * heating
            dr = carried(r)
            return [sea * d for d in (du, dv, dq, dr)]

        def ocean_step():
            for k in range(levels):
                start = [grid[f * levels + k] for f in range(4)]
                heating = grid[first_heat + k]
                first = [s + DT_OCEAN * d for s, d in zip(start, rates(*start, heating, k))]
                second = [
                    0.75 * s + 0.25 * (f + DT_OCEAN * d)
                    for s, f, d in zip(start, first, rates(*first, heating, k))
                ]
                third = [
                    ONE_THIRD * s + TWO_THIRDS * (f + DT_OCEAN * d)
                    for s, f, d in zip(start, second, rates(*second, heating, k))
                ]
                for f in range(4):
                    grid[f * levels + k] = third[f]

        def column_fields():
            total = None
            for k in range(levels - 1, 0, -1):
                u, v = grid[k], grid[levels + k]
                east = pltpu.roll(u, padded_rows - 1, 0)
                west = pltpu.roll(u, 1, 0)
                north = jnp.where(not_last, pltpu.roll(v, lat - 1, 1), 0.0)
                south = jnp.where(not_first, pltpu.roll(v, 1, 1), 0.0)
                div = 0.5 * (east - west) + 0.5 * (north - south)
                total = div if total is None else total + div
                fields[k - 1] = W_LIMIT * jnp.tanh(W_GAIN * total)
                shear = (u - grid[k - 1]) ** 2 + (v - grid[levels + k - 1]) ** 2
                fields[levels - 1 + k - 1] = KV_BASE + KV_SHEAR * shear / (1.0 + shear)

        fields[2 * (levels - 1)] = (
            grid[first_wind] * grid[first_wind] + grid[first_wind + 1] * grid[first_wind + 1]
        )

        def sent_channels():
            refs = [(grid, 2 * levels + i) for i in range(2 * levels)]
            refs += [(fields, i) for i in range(2 * levels - 1)]
            refs += [(grid, sun_row)]
            return refs

        tile_count = ceil_to(width, 8) // 8
        sublane = lax.broadcasted_iota(jnp.int32, (8, LANES), 0)

        def field_copy(step, h, slot):
            return pltpu.make_async_remote_copy(
                src_ref=send.at[step, h],
                dst_ref=recv.at[step, slot],
                send_sem=field_ssem.at[step, h],
                recv_sem=field_rsem.at[step, slot],
                device_id=(sec, h),
                device_id_type=MESH,
            )

        def pick(step, h):
            listed = lists_ref[pl.ds((sec - 1) * strips + h, 1), :]
            x = jnp.broadcast_to(listed >> lat_shift, (8, LANES))
            y = jnp.broadcast_to(listed & (lat - 1), (8, LANES))
            low = y & (LANES - 1)
            half = y >> (LANES.bit_length() - 1)
            for c, (ref, row) in enumerate(sent_channels()):
                total = jnp.zeros((8, LANES), jnp.float32)
                for tile in range(tile_count):
                    rows = slice(HALO + 8 * tile, HALO + 8 * tile + 8)
                    for part in range(halves):
                        taken = jnp.take_along_axis(
                            ref[row, rows, part * LANES : (part + 1) * LANES],
                            low,
                            axis=1,
                            mode="promise_in_bounds",
                        )
                        mine = (x == sublane + 8 * tile) & (half == part)
                        total = jnp.where(mine, taken, total)
                send[step, h, c : c + 1, :] = jnp.sum(total, axis=0, keepdims=True)

        def send_fields(step):
            def one(i, carry):
                h = lax.rem(strip + i, strips)
                pick(step, h)
                field_copy(step, h, strip).start()
                return carry

            lax.fori_loop(1, strips, one, 0)
            pick(step, strip)
            recv[step, strip] = send[step, strip]

        def wait_fields(step):
            def one(i, carry):
                h = lax.rem(strip + i, strips)
                field_copy(step, h, h).wait()
                return carry

            lax.fori_loop(1, strips, one, 0)

        def advance(step, source, last):
            def received(c):
                return jnp.concatenate(
                    [recv[step, h, c : c + 1, :] for h in range(strips)], axis=0
                )

            heat_now = [received(k) for k in range(levels)]
            salt_top = received(levels)
            base = 2 * levels
            weights = transport_weights(
                [None] + [received(base + k) for k in range(levels - 1)]
            )
            mixing = [None] + [received(base + levels - 1 + k) for k in range(levels - 1)]
            power = received(base + 2 * (levels - 1))
            sunlight = received(ROWS_SENT - 1)
            valid = sunlight > 0.5
            transfer = GAS_RATE * power / (1.0 + power)

            before = [[source[n, k] for k in range(levels)] for n in range(4)]
            moved = [transport(column, weights, mixing) for column in before]
            mids, heats = light_profile(moved[1], sunlight)
            surplus = []
            for k in range(levels):
                n_, p_, z_, d_ = (moved[i][k] for i in range(4))
                warm = jnp.exp(HEATUP_PER_STEP * heat_now[k])
                growth = (
                    GROWTH * warm * mids[k] / (mids[k] + 1.0) * jnp.abs(n_) / (jnp.abs(n_) + 1.0) * p_
                )
                grazing = GRAZING * warm * p_ * p_ / (p_ * p_ + 1.0) * z_
                remineral = REMINERAL * warm * d_
                changes = (
                    -growth + remineral + EXCRETION * z_,
                    growth - grazing - PHYTO_LOSS * p_,
                    ASSIMILATE * grazing - EXCRETION * z_ - ZOO_LOSS * z_,
                    (1.0 - ASSIMILATE) * grazing + PHYTO_LOSS * p_ + ZOO_LOSS * z_ - remineral,
                )
                for i in range(4):
                    out_c[i, k] = jnp.where(
                        valid, moved[i][k] + DT_BIO * changes[i], before[i][k]
                    )
                surplus.append(remineral - growth)
                if last:
                    out_h[k] = jnp.where(valid, heats[k], 0.0)
            for n in range(4, species):
                column = [source[n, k] for k in range(levels)]
                now = transport(column, weights, mixing)
                if GAS_ON[n]:
                    limit = (
                        float(SOLUBILITY_BASE[n])
                        + float(SOLUBILITY_HEAT[n]) * heat_now[0]
                        + float(SOLUBILITY_BRINE[n]) * salt_top
                    )
                    now[0] = now[0] + DT_BIO * transfer * (limit - now[0])
                for k in range(levels):
                    change = float(YIELDS[n]) * surplus[k] - float(DECAYS[n]) * now[k]
                    out_c[n, k] = jnp.where(valid, now[k] + DT_BIO * change, column[k])

        for step in range(STEPS):
            ocean_step()
            column_fields()
            send_fields(step)
            if step == 0:
                for copy in rim_copies:
                    copy.wait()
                for k in range(levels):
                    phyto_grid[k, HALO - 2 : HALO, :] = rim_in[0, 2 * k : 2 * k + 2, :]
                    phyto_grid[k, HALO + width : HALO + width + 2, :] = rim_in[
                        1, 2 * k : 2 * k + 2, :
                    ]
                weights = transport_weights([None] + [fields[k] for k in range(levels - 1)])
                mixing = [None] + [fields[levels - 1 + k] for k in range(levels - 1)]
                moved = transport([phyto_grid[k] for k in range(levels)], weights, mixing)
                _, heats = light_profile(moved, grid[sun_row])
                for k in range(levels):
                    grid[first_heat + k] = heats[k]
        wait_fields(0)
        advance(0, trac_ref, False)
        wait_fields(1)
        advance(1, out_c, True)


def per_device(ocean_state, heat_first, wind_stress, shortwave, sea_mask, owner_cols, tracers):
    sections = lax.axis_size("sec")
    strips = lax.axis_size("gx")
    fields_count, levels, width, lat = ocean_state.shape
    owners = (sections - 1) * strips
    species = tracers.shape[0]
    padded_rows = ceil_to(width + 2 * HALO, 8)
    place_rows = ceil_to(width, 16)
    channels = 5 * levels + 4
    f32 = jnp.float32
    vmem = pl.BlockSpec(memory_space=pltpu.VMEM)
    new_c, new_h = pl.pallas_call(
        functools.partial(whole_kernel, sections, strips, levels, width, lat),
        out_shape=(
            jax.ShapeDtypeStruct((species, levels, strips, LANES), f32),
            jax.ShapeDtypeStruct((levels, strips, LANES), f32),
        ),
        in_specs=[vmem] * 8,
        out_specs=(vmem, vmem),
        scratch_shapes=[
            pltpu.VMEM((channels, padded_rows, lat), f32),
            pltpu.VMEM((2, channels, HALO, lat), f32),
            pltpu.VMEM((2, channels, HALO, lat), f32),
            pltpu.VMEM((owners, levels, LANES), f32),
            pltpu.VMEM((3 * levels * place_rows, owners * LANES), jnp.bfloat16),
            pltpu.VMEM((lat, owners * LANES), jnp.bfloat16),
            pltpu.VMEM((levels, padded_rows, lat), f32),
            pltpu.VMEM((2, 2 * levels, lat), f32),
            pltpu.VMEM((2, 2 * levels, lat), f32),
            pltpu.VMEM((2 * levels - 1, padded_rows, lat), f32),
            pltpu.VMEM((STEPS, strips, ROWS_SENT, LANES), f32),
            pltpu.VMEM((STEPS, strips, ROWS_SENT, LANES), f32),
            pltpu.SemaphoreType.DMA((2,)),
            pltpu.SemaphoreType.DMA((2,)),
            pltpu.SemaphoreType.DMA((owners,)),
            pltpu.SemaphoreType.DMA((owners,)),
            pltpu.SemaphoreType.DMA((2,)),
            pltpu.SemaphoreType.DMA((2,)),
            pltpu.SemaphoreType.DMA((STEPS, strips)),
            pltpu.SemaphoreType.DMA((STEPS, strips)),
        ],
        compiler_params=pltpu.CompilerParams(
            collective_id=0, has_side_effects=True, vmem_limit_bytes=56 << 20
        ),
    )(
        ocean_state.reshape(fields_count * levels, width, lat),
        heat_first,
        wind_stress,
        shortwave,
        sea_mask,
        owner_cols.reshape(owners, LANES),
        tracers[1],
        tracers.reshape(species, levels, strips, LANES),
    )
    return new_c.reshape(tracers.shape), new_h.reshape(levels, -1)


def solution(mesh):
    return jax.shard_map(
        per_device,
        mesh=mesh,
        in_specs=(
            P(None, None, "gx", None),
            P(None, "gx", None),
            P(None, "gx", None),
            P("gx", None),
            P("gx", None),
            P("gx", None, None, None),
            P(None, None, ("sec", "gx")),
        ),
        out_specs=(P(None, None, ("sec", "gx")), P(None, ("sec", "gx"))),
        check_vma=False,
    )
```

```python
import functools

import jax
import jax.numpy as jnp
import numpy as np
from jax import lax
from jax.experimental import pallas as pl
from jax.experimental.pallas import tpu as pltpu
from jax.sharding import PartitionSpec as P

STEPS = 2


DT_OCEAN = 0.15
VISCOSITY = 0.2
DIFFUSIVITY = 0.15
DAMPING = 0.05
CORIOLIS = 0.8
HEAT_GAIN = 4.0
ONE_THIRD = 1.0 / 3.0
TWO_THIRDS = 2.0 / 3.0
DT_BIO = 0.8
W_LIMIT = 0.35
W_GAIN = 0.25
KV_BASE = 0.05
KV_SHEAR = 0.3
GAS_RATE = 0.5
WATER_ATTEN = 0.15
CHLORO_ATTEN = 0.1
HEATUP_PER_STEP = 0.5
GROWTH = 0.6
GRAZING = 0.4
REMINERAL = 0.2
EXCRETION = 0.1
PHYTO_LOSS = 0.05
ZOO_LOSS = 0.05
ASSIMILATE = 0.6
YIELDS = np.array(
    [
        0.0,
        0.0,
        0.0,
        0.0,
        -1.3,
        1.0,
        0.16,
        0.9,
        -0.6,
        0.4,
        1.2,
        -0.8,
        0.5,
        0.3,
        -0.4,
        0.7,
        -1.0,
        0.2,
        0.6,
    ],
    np.float32,
)
DECAYS = np.array(
    [
        0.0,
        0.0,
        0.0,
        0.0,
        0.02,
        0.01,
        0.05,
        0.03,
        0.08,
        0.04,
        0.02,
        0.06,
        0.1,
        0.03,
        0.07,
        0.05,
        0.02,
        0.09,
        0.04,
    ],
    np.float32,
)
GAS_ON = np.array([0, 0, 0, 0, 1, 1] + [0] * 13, np.float32)
SOLUBILITY_BASE = np.array([0, 0, 0, 0, 1.2, 1.0] + [0] * 13, np.float32)
SOLUBILITY_HEAT = np.array([0, 0, 0, 0, -0.5, -0.3] + [0] * 13, np.float32)
SOLUBILITY_BRINE = np.array([0, 0, 0, 0, 0.1, 0.3] + [0] * 13, np.float32)

MESH = pl.DeviceIdType.MESH
HALO = 8
LANES = 128
ROWS_SENT = 16


def minmod(one_side, other_side):
    return jnp.maximum(0.0, jnp.minimum(one_side, other_side)) + jnp.minimum(
        0.0, jnp.maximum(one_side, other_side)
    )


def transport_weights(upwelling):
    return [
        None
        if w is None
        else (jnp.maximum(w, 0.0), jnp.minimum(w, 0.0), 0.5 * (1.0 - DT_BIO * jnp.abs(w)))
        for w in upwelling
    ]


def transport(column, weights, mixing):
    levels = len(column)
    diffs = [column[k + 1] - column[k] for k in range(levels - 1)]
    slopes = [None] + [minmod(diffs[k], diffs[k - 1]) for k in range(1, levels - 1)] + [None]
    flux = [None] * (levels + 1)
    for k in range(1, levels):
        up, down, half = weights[k]
        from_below = column[k] if slopes[k] is None else column[k] - half * slopes[k]
        from_above = column[k - 1] if slopes[k - 1] is None else column[k - 1] + half * slopes[k - 1]
        flux[k] = up * from_below + down * from_above + mixing[k] * diffs[k - 1]
    out = []
    for k in range(levels):
        if k == 0:
            gain = flux[1]
        elif k == levels - 1:
            gain = -flux[k]
        else:
            gain = flux[k + 1] - flux[k]
        out.append(column[k] + DT_BIO * gain)
    return out


def light_profile(phyto, sunlight):
    mids, heats = [], []
    top = sunlight
    for p in phyto:
        extinction = WATER_ATTEN + CHLORO_ATTEN * jnp.abs(p)
        mid_pass = jnp.exp(-0.5 * extinction)
        mids.append(top * mid_pass)
        after = top * jnp.exp(-extinction)
        heats.append(top - after)
        top = after
    return mids, heats


def ceil_to(value, unit):
    return (value + unit - 1) // unit * unit


def whole_kernel(
    sections,
    strips,
    levels,
    width,
    lat,
    state_ref,
    heat_ref,
    wind_ref,
    sun_ref,
    sea_ref,
    lists_ref,
    trac_ref,
    out_c,
    out_h,
    grid,
    halo_out,
    halo_in,
    phyto_out,
    phyto_in,
    placed,
    onehot,
    phyto_grid,
    rim_out,
    rim_in,
    fields,
    send,
    recv,
    halo_ssem,
    halo_rsem,
    phyto_ssem,
    phyto_rsem,
    rim_ssem,
    rim_rsem,
    field_ssem,
    field_rsem,
):
    owners = (sections - 1) * strips
    species = trac_ref.shape[0]
    padded_rows = grid.shape[1]
    sec = lax.axis_index("sec")
    strip = lax.axis_index("gx")
    right = lax.rem(strip + 1, strips)
    left = lax.rem(strip + strips - 1, strips)
    me = (sec - 1) * strips + strip
    lat_shift = lat.bit_length() - 1
    halves = lat // LANES
    place_rows = placed.shape[0] // (3 * levels)
    first_heat = 4 * levels
    first_wind = 5 * levels
    sun_row = first_wind + 2
    sea_row = first_wind + 3

    @pl.when(sec == 0)
    def _():
        out_c[...] = trac_ref[...]
        out_h[...] = jnp.zeros_like(out_h)

    @pl.when(sec > 0)
    def _():
        def channel(c, rows):
            count = rows.stop - rows.start

            def interleaved(ref, lead, group, member):
                return jnp.concatenate(
                    [
                        ref[
                            pl.ds(
                                ((lead * width + rows.start) * halves + part) * group + member,
                                count,
                                stride=halves * group,
                            ),
                            :,
                        ]
                        for part in range(halves)
                    ],
                    axis=1,
                )

            if c < first_heat:
                return interleaved(state_ref, c // levels, levels, c % levels)
            if c < first_wind:
                return interleaved(heat_ref, 0, levels, c - first_heat)
            if c < sun_row:
                return interleaved(wind_ref, 0, 2, c - first_wind)
            if c == sun_row:
                return sun_ref[rows, :]
            return sea_ref[rows, :].astype(jnp.float32)

        for c in range(grid.shape[0]):
            halo_out[0, c] = channel(c, slice(width - HALO, width))
            halo_out[1, c] = channel(c, slice(0, HALO))

        for h in range(strips):
            phyto_out[h] = trac_ref[1, h * levels : (h + 1) * levels, :]

        barrier = pltpu.get_barrier_semaphore()

        def greet(i, carry):
            t = lax.rem(me + i, owners)
            pl.semaphore_signal(
                barrier, inc=1, device_id=(1 + t // strips, lax.rem(t, strips)), device_id_type=MESH
            )
            return carry

        lax.fori_loop(1, owners, greet, 0)
        pl.semaphore_wait(barrier, owners - 1)

        def edge_copy(out_ref, in_ref, ssem, rsem, side):
            return pltpu.make_async_remote_copy(
                src_ref=out_ref.at[side],
                dst_ref=in_ref.at[side],
                send_sem=ssem.at[side],
                recv_sem=rsem.at[side],
                device_id=(sec, right if side == 0 else left),
                device_id_type=MESH,
            )

        halo_copies = [
            edge_copy(halo_out, halo_in, halo_ssem, halo_rsem, side) for side in range(2)
        ]

        def phyto_copy(t, slot):
            target = lax.rem(t, strips)
            return pltpu.make_async_remote_copy(
                src_ref=phyto_out.at[target],
                dst_ref=phyto_in.at[slot],
                send_sem=phyto_ssem.at[t],
                recv_sem=phyto_rsem.at[slot],
                device_id=(1 + t // strips, target),
                device_id_type=MESH,
            )

        def send_phyto(i, carry):
            phyto_copy(lax.rem(me + i, owners), me).start()
            return carry

        lax.fori_loop(1, owners, send_phyto, 0)
        for copy in halo_copies:
            copy.start()

        phyto_in[me] = phyto_out[strip]

        for c in range(grid.shape[0]):
            if padded_rows > width + 2 * HALO:
                grid[c, width + 2 * HALO :, :] = jnp.zeros(
                    (padded_rows - width - 2 * HALO, lat), jnp.float32
                )
            grid[c, HALO : HALO + width, :] = channel(c, slice(0, width))

        def wait_phyto(i, carry):
            t = lax.rem(me + i, owners)
            phyto_copy(t, t).wait()
            return carry

        lax.fori_loop(1, owners, wait_phyto, 0)

        lat_index = lax.broadcasted_iota(jnp.int32, (lat, LANES), 0)
        lon_index = lax.broadcasted_iota(jnp.int32, (place_rows, LANES), 0)

        def spread(l, carry):
            listed = lists_ref[pl.ds(l, 1), :]
            x = listed >> lat_shift
            y = listed & (lat - 1)
            lanes = pl.ds(pl.multiple_of(l * LANES, LANES), LANES)
            onehot[:, lanes] = jnp.where(lat_index == y, 1.0, 0.0).astype(jnp.bfloat16)
            here = lon_index == x
            values = phyto_in[l]
            for k in range(levels):
                rest = values[k : k + 1, :]
                for part in range(3):
                    term = rest.astype(jnp.bfloat16).astype(jnp.float32)
                    rest = rest - term
                    row = (3 * k + part) * place_rows
                    placed[row : row + place_rows, lanes] = jnp.where(here, term, 0.0).astype(
                        jnp.bfloat16
                    )
            return carry

        lax.fori_loop(0, owners, spread, 0)
        spread_out = lax.dot_general(
            placed[...],
            onehot[...],
            (((1,), (1,)), ((), ())),
            preferred_element_type=jnp.float32,
        )
        for k in range(levels):
            base = 3 * k * place_rows
            own = (
                spread_out[base : base + width]
                + spread_out[base + place_rows : base + place_rows + width]
                + spread_out[base + 2 * place_rows : base + 2 * place_rows + width]
            )
            phyto_grid[k] = jnp.zeros((padded_rows, lat), jnp.float32)
            phyto_grid[k, HALO : HALO + width, :] = own
            rim_out[0, 2 * k : 2 * k + 2, :] = own[width - 2 : width]
            rim_out[1, 2 * k : 2 * k + 2, :] = own[0:2]

        rim_copies = [edge_copy(rim_out, rim_in, rim_ssem, rim_rsem, side) for side in range(2)]
        for copy in rim_copies:
            copy.start()
        for copy in halo_copies:
            copy.wait()
        for c in range(grid.shape[0]):
            grid[c, 0:HALO, :] = halo_in[0, c]
            grid[c, HALO + width : 2 * HALO + width, :] = halo_in[1, c]

        lane = lax.broadcasted_iota(jnp.int32, (padded_rows, lat), 1)
        not_last = lane < lat - 1
        not_first = lane > 0
        coriolis_y = CORIOLIS * (2.0 * (lane.astype(jnp.float32) + 0.5) / lat - 1.0)

        def around(field):
            east = pltpu.roll(field, padded_rows - 1, 0)
            west = pltpu.roll(field, 1, 0)
            north = jnp.where(not_last, pltpu.roll(field, lat - 1, 1), 0.0)
            south = jnp.where(not_first, pltpu.roll(field, 1, 1), 0.0)
            return east, west, north, south

        def rates(u, v, q, r, heating, k):
            def flow(field):
                east, west, north, south = around(field)
                return east + west + north + south - 4.0 * field

            def carried(field):
                east, west, north, south = around(field)
                return (
                    DIFFUSIVITY * (east + west + north + south - 4.0 * field)
                    - (u * (0.5 * (east - west)) + v * (0.5 * (north - south)))
                )

            sea = grid[sea_row]
            du = coriolis_y * v - DAMPING * u + VISCOSITY * flow(u)
            dv = -coriolis_y * u - DAMPING * v + VISCOSITY * flow(v)
            if k == 0:
                du = du + grid[first_wind]
                dv = dv + grid[first_wind + 1]
            dq = carried(q) + HEAT_GAIN * heating
            dr = carried(r)
            return [sea * d for d in (du, dv, dq, dr)]

        def ocean_step():
            for k in range(levels):
                start = [grid[f * levels + k] for f in range(4)]
                heating = grid[first_heat + k]
                first = [s + DT_OCEAN * d for s, d in zip(start, rates(*start, heating, k))]
                second = [
                    0.75 * s + 0.25 * (f + DT_OCEAN * d)
                    for s, f, d in zip(start, first, rates(*first, heating, k))
                ]
                third = [
                    ONE_THIRD * s + TWO_THIRDS * (f + DT_OCEAN * d)
                    for s, f, d in zip(start, second, rates(*second, heating, k))
                ]
                for f in range(4):
                    grid[f * levels + k] = third[f]

        def column_fields():
            total = None
            for k in range(levels - 1, 0, -1):
                u, v = grid[k], grid[levels + k]
                east = pltpu.roll(u, padded_rows - 1, 0)
                west = pltpu.roll(u, 1, 0)
                north = jnp.where(not_last, pltpu.roll(v, lat - 1, 1), 0.0)
                south = jnp.where(not_first, pltpu.roll(v, 1, 1), 0.0)
                div = 0.5 * (east - west) + 0.5 * (north - south)
                total = div if total is None else total + div
                fields[k - 1] = W_LIMIT * jnp.tanh(W_GAIN * total)
                shear = (u - grid[k - 1]) ** 2 + (v - grid[levels + k - 1]) ** 2
                fields[levels - 1 + k - 1] = KV_BASE + KV_SHEAR * shear / (1.0 + shear)

        fields[2 * (levels - 1)] = (
            grid[first_wind] * grid[first_wind] + grid[first_wind + 1] * grid[first_wind + 1]
        )

        def sent_channels():
            refs = [(grid, 2 * levels + i) for i in range(2 * levels)]
            refs += [(fields, i) for i in range(2 * levels - 1)]
            refs += [(grid, sun_row)]
            return refs

        tile_count = ceil_to(width, 8) // 8
        sublane = lax.broadcasted_iota(jnp.int32, (8, LANES), 0)

        def field_copy(step, h, slot):
            return pltpu.make_async_remote_copy(
                src_ref=send.at[step, h],
                dst_ref=recv.at[
                    step, pl.ds(pl.multiple_of(slot * ROWS_SENT, ROWS_SENT), ROWS_SENT)
                ],
                send_sem=field_ssem.at[step, h],
                recv_sem=field_rsem.at[step, slot],
                device_id=(sec, h),
                device_id_type=MESH,
            )

        def pick(step, h):
            listed = lists_ref[pl.ds((sec - 1) * strips + h, 1), :]
            x = jnp.broadcast_to(listed >> lat_shift, (8, LANES))
            y = jnp.broadcast_to(listed & (lat - 1), (8, LANES))
            low = y & (LANES - 1)
            half = y >> (LANES.bit_length() - 1)
            for c, (ref, row) in enumerate(sent_channels()):
                total = jnp.zeros((8, LANES), jnp.float32)
                for tile in range(tile_count):
                    rows = slice(HALO + 8 * tile, HALO + 8 * tile + 8)
                    for part in range(halves):
                        taken = jnp.take_along_axis(
                            ref[row, rows, part * LANES : (part + 1) * LANES],
                            low,
                            axis=1,
                            mode="promise_in_bounds",
                        )
                        mine = (x == sublane + 8 * tile) & (half == part)
                        total = jnp.where(mine, taken, total)
                send[step, h, c : c + 1, :] = jnp.sum(total, axis=0, keepdims=True)

        def send_fields(step):
            def one(i, carry):
                h = lax.rem(strip + i, strips)
                pick(step, h)
                field_copy(step, h, strip).start()
                return carry

            lax.fori_loop(1, strips, one, 0)
            pick(step, strip)
            recv[step, pl.ds(pl.multiple_of(strip * ROWS_SENT, ROWS_SENT), ROWS_SENT), :] = send[
                step, strip
            ]

        def wait_fields(step):
            def one(i, carry):
                h = lax.rem(strip + i, strips)
                field_copy(step, h, h).wait()
                return carry

            lax.fori_loop(1, strips, one, 0)

        def advance(step, source, last):
            def received(c):
                return recv[step, pl.ds(c, strips, stride=ROWS_SENT), :]

            def level_rows(k):
                return pl.ds(k, strips, stride=levels)

            heat_now = [received(k) for k in range(levels)]
            salt_top = received(levels)
            base = 2 * levels
            weights = transport_weights(
                [None] + [received(base + k) for k in range(levels - 1)]
            )
            mixing = [None] + [received(base + levels - 1 + k) for k in range(levels - 1)]
            power = received(base + 2 * (levels - 1))
            sunlight = received(ROWS_SENT - 1)
            valid = sunlight > 0.5
            transfer = GAS_RATE * power / (1.0 + power)

            before = [[source[n, level_rows(k), :] for k in range(levels)] for n in range(4)]
            moved = [transport(column, weights, mixing) for column in before]
            mids, heats = light_profile(moved[1], sunlight)
            surplus = []
            for k in range(levels):
                n_, p_, z_, d_ = (moved[i][k] for i in range(4))
                warm = jnp.exp(HEATUP_PER_STEP * heat_now[k])
                growth = (
                    GROWTH * warm * mids[k] / (mids[k] + 1.0) * jnp.abs(n_) / (jnp.abs(n_) + 1.0) * p_
                )
                grazing = GRAZING * warm * p_ * p_ / (p_ * p_ + 1.0) * z_
                remineral = REMINERAL * warm * d_
                changes = (
                    -growth + remineral + EXCRETION * z_,
                    growth - grazing - PHYTO_LOSS * p_,
                    ASSIMILATE * grazing - EXCRETION * z_ - ZOO_LOSS * z_,
                    (1.0 - ASSIMILATE) * grazing + PHYTO_LOSS * p_ + ZOO_LOSS * z_ - remineral,
                )
                for i in range(4):
                    out_c[i, level_rows(k), :] = jnp.where(
                        valid, moved[i][k] + DT_BIO * changes[i], before[i][k]
                    )
                surplus.append(remineral - growth)
                if last:
                    out_h[level_rows(k), :] = jnp.where(valid, heats[k], 0.0)
            for n in range(4, species):
                column = [source[n, level_rows(k), :] for k in range(levels)]
                now = transport(column, weights, mixing)
                if GAS_ON[n]:
                    limit = (
                        float(SOLUBILITY_BASE[n])
                        + float(SOLUBILITY_HEAT[n]) * heat_now[0]
                        + float(SOLUBILITY_BRINE[n]) * salt_top
                    )
                    now[0] = now[0] + DT_BIO * transfer * (limit - now[0])
                for k in range(levels):
                    change = float(YIELDS[n]) * surplus[k] - float(DECAYS[n]) * now[k]
                    out_c[n, level_rows(k), :] = jnp.where(valid, now[k] + DT_BIO * change, column[k])

        for step in range(STEPS):
            ocean_step()
            column_fields()
            send_fields(step)
            if step == 0:
                for copy in rim_copies:
                    copy.wait()
                for k in range(levels):
                    phyto_grid[k, HALO - 2 : HALO, :] = rim_in[0, 2 * k : 2 * k + 2, :]
                    phyto_grid[k, HALO + width : HALO + width + 2, :] = rim_in[
                        1, 2 * k : 2 * k + 2, :
                    ]
                weights = transport_weights([None] + [fields[k] for k in range(levels - 1)])
                mixing = [None] + [fields[levels - 1 + k] for k in range(levels - 1)]
                moved = transport([phyto_grid[k] for k in range(levels)], weights, mixing)
                _, heats = light_profile(moved, grid[sun_row])
                for k in range(levels):
                    grid[first_heat + k] = heats[k]
        wait_fields(0)
        advance(0, trac_ref, False)
        wait_fields(1)
        advance(1, out_c, True)


def per_device(ocean_state, heat_first, wind_stress, shortwave, sea_mask, owner_cols, tracers):
    sections = lax.axis_size("sec")
    strips = lax.axis_size("gx")
    fields_count, levels, width, lat = ocean_state.shape
    owners = (sections - 1) * strips
    species = tracers.shape[0]
    padded_rows = ceil_to(width + 2 * HALO, 8)
    place_rows = ceil_to(width, 16)
    channels = 5 * levels + 4
    halves = lat // LANES
    f32 = jnp.float32
    vmem = pl.BlockSpec(memory_space=pltpu.VMEM)
    new_c, new_h = pl.pallas_call(
        functools.partial(whole_kernel, sections, strips, levels, width, lat),
        out_shape=(
            jax.ShapeDtypeStruct((species, strips * levels, LANES), f32),
            jax.ShapeDtypeStruct((strips * levels, LANES), f32),
        ),
        in_specs=[vmem] * 7,
        out_specs=(vmem, vmem),
        scratch_shapes=[
            pltpu.VMEM((channels, padded_rows, lat), f32),
            pltpu.VMEM((2, channels, HALO, lat), f32),
            pltpu.VMEM((2, channels, HALO, lat), f32),
            pltpu.VMEM((strips, levels, LANES), f32),
            pltpu.VMEM((owners, levels, LANES), f32),
            pltpu.VMEM((3 * levels * place_rows, owners * LANES), jnp.bfloat16),
            pltpu.VMEM((lat, owners * LANES), jnp.bfloat16),
            pltpu.VMEM((levels, padded_rows, lat), f32),
            pltpu.VMEM((2, 2 * levels, lat), f32),
            pltpu.VMEM((2, 2 * levels, lat), f32),
            pltpu.VMEM((2 * levels - 1, padded_rows, lat), f32),
            pltpu.VMEM((STEPS, strips, ROWS_SENT, LANES), f32),
            pltpu.VMEM((STEPS, strips * ROWS_SENT, LANES), f32),
            pltpu.SemaphoreType.DMA((2,)),
            pltpu.SemaphoreType.DMA((2,)),
            pltpu.SemaphoreType.DMA((owners,)),
            pltpu.SemaphoreType.DMA((owners,)),
            pltpu.SemaphoreType.DMA((2,)),
            pltpu.SemaphoreType.DMA((2,)),
            pltpu.SemaphoreType.DMA((STEPS, strips)),
            pltpu.SemaphoreType.DMA((STEPS, strips)),
        ],
        compiler_params=pltpu.CompilerParams(
            collective_id=0, has_side_effects=True, vmem_limit_bytes=56 << 20
        ),
    )(
        ocean_state.reshape(fields_count, levels, width, halves, LANES)
        .transpose(0, 2, 3, 1, 4)
        .reshape(-1, LANES),
        heat_first.reshape(levels, width, halves, LANES).transpose(1, 2, 0, 3).reshape(-1, LANES),
        wind_stress.reshape(2, width, halves, LANES).transpose(1, 2, 0, 3).reshape(-1, LANES),
        shortwave,
        sea_mask,
        owner_cols.reshape(owners, LANES),
        tracers.reshape(species, levels, strips, LANES)
        .transpose(0, 2, 1, 3)
        .reshape(species, strips * levels, LANES),
    )
    new_c = new_c.reshape(species, strips, levels, LANES).transpose(0, 2, 1, 3)
    new_h = new_h.reshape(strips, levels, LANES).transpose(1, 0, 2)
    return new_c.reshape(tracers.shape), new_h.reshape(levels, -1)


def solution(mesh):
    return jax.shard_map(
        per_device,
        mesh=mesh,
        in_specs=(
            P(None, None, "gx", None),
            P(None, "gx", None),
            P(None, "gx", None),
            P("gx", None),
            P("gx", None),
            P("gx", None, None, None),
            P(None, None, ("sec", "gx")),
        ),
        out_specs=(P(None, None, ("sec", "gx")), P(None, ("sec", "gx"))),
        check_vma=False,
    )
```

```python
import functools

import jax
import jax.numpy as jnp
import numpy as np
from jax import lax
from jax.experimental import pallas as pl
from jax.experimental.pallas import tpu as pltpu
from jax.sharding import PartitionSpec as P

STEPS = 2


DT_OCEAN = 0.15
VISCOSITY = 0.2
DIFFUSIVITY = 0.15
DAMPING = 0.05
CORIOLIS = 0.8
HEAT_GAIN = 4.0
ONE_THIRD = 1.0 / 3.0
TWO_THIRDS = 2.0 / 3.0
DT_BIO = 0.8
W_LIMIT = 0.35
W_GAIN = 0.25
KV_BASE = 0.05
KV_SHEAR = 0.3
GAS_RATE = 0.5
WATER_ATTEN = 0.15
CHLORO_ATTEN = 0.1
HEATUP_PER_STEP = 0.5
GROWTH = 0.6
GRAZING = 0.4
REMINERAL = 0.2
EXCRETION = 0.1
PHYTO_LOSS = 0.05
ZOO_LOSS = 0.05
ASSIMILATE = 0.6
YIELDS = np.array(
    [
        0.0,
        0.0,
        0.0,
        0.0,
        -1.3,
        1.0,
        0.16,
        0.9,
        -0.6,
        0.4,
        1.2,
        -0.8,
        0.5,
        0.3,
        -0.4,
        0.7,
        -1.0,
        0.2,
        0.6,
    ],
    np.float32,
)
DECAYS = np.array(
    [
        0.0,
        0.0,
        0.0,
        0.0,
        0.02,
        0.01,
        0.05,
        0.03,
        0.08,
        0.04,
        0.02,
        0.06,
        0.1,
        0.03,
        0.07,
        0.05,
        0.02,
        0.09,
        0.04,
    ],
    np.float32,
)
GAS_ON = np.array([0, 0, 0, 0, 1, 1] + [0] * 13, np.float32)
SOLUBILITY_BASE = np.array([0, 0, 0, 0, 1.2, 1.0] + [0] * 13, np.float32)
SOLUBILITY_HEAT = np.array([0, 0, 0, 0, -0.5, -0.3] + [0] * 13, np.float32)
SOLUBILITY_BRINE = np.array([0, 0, 0, 0, 0.1, 0.3] + [0] * 13, np.float32)

MESH = pl.DeviceIdType.MESH
HALO = 8
LANES = 128
ROWS_SENT = 16


def minmod(one_side, other_side):
    return jnp.maximum(0.0, jnp.minimum(one_side, other_side)) + jnp.minimum(
        0.0, jnp.maximum(one_side, other_side)
    )


def transport_weights(upwelling):
    return [
        None
        if w is None
        else (jnp.maximum(w, 0.0), jnp.minimum(w, 0.0), 0.5 * (1.0 - DT_BIO * jnp.abs(w)))
        for w in upwelling
    ]


def transport(column, weights, mixing):
    levels = len(column)
    diffs = [column[k + 1] - column[k] for k in range(levels - 1)]
    slopes = [None] + [minmod(diffs[k], diffs[k - 1]) for k in range(1, levels - 1)] + [None]
    flux = [None] * (levels + 1)
    for k in range(1, levels):
        up, down, half = weights[k]
        from_below = column[k] if slopes[k] is None else column[k] - half * slopes[k]
        from_above = column[k - 1] if slopes[k - 1] is None else column[k - 1] + half * slopes[k - 1]
        flux[k] = up * from_below + down * from_above + mixing[k] * diffs[k - 1]
    out = []
    for k in range(levels):
        if k == 0:
            gain = flux[1]
        elif k == levels - 1:
            gain = -flux[k]
        else:
            gain = flux[k + 1] - flux[k]
        out.append(column[k] + DT_BIO * gain)
    return out


def light_profile(phyto, sunlight):
    mids, heats = [], []
    top = sunlight
    for p in phyto:
        extinction = WATER_ATTEN + CHLORO_ATTEN * jnp.abs(p)
        mid_pass = jnp.exp(-0.5 * extinction)
        mids.append(top * mid_pass)
        after = top * jnp.exp(-extinction)
        heats.append(top - after)
        top = after
    return mids, heats


def ceil_to(value, unit):
    return (value + unit - 1) // unit * unit


def ocean_kernel(
    sections,
    strips,
    levels,
    width,
    lat,
    state_ref,
    heat_ref,
    wind_ref,
    sun_ref,
    sea_ref,
    lists_ref,
    trac_ref,
    received_ref,
    grid,
    halo_out,
    halo_in,
    phyto_own,
    phyto_out,
    phyto_in,
    placed,
    onehot,
    phyto_grid,
    rim_out,
    rim_in,
    fields,
    send,
    recv,
    own_sem,
    halo_ssem,
    halo_rsem,
    pass_ssem,
    pass_rsem,
    phyto_ssem,
    phyto_rsem,
    rim_ssem,
    rim_rsem,
    field_ssem,
    field_rsem,
):
    owners = (sections - 1) * strips
    padded_rows = grid.shape[1]
    sec = lax.axis_index("sec")
    strip = lax.axis_index("gx")
    right = lax.rem(strip + 1, strips)
    left = lax.rem(strip + strips - 1, strips)
    me = (sec - 1) * strips + strip
    lat_shift = lat.bit_length() - 1
    halves = lat // LANES
    place_rows = placed.shape[0] // (3 * levels)
    first_heat = 4 * levels
    first_wind = 5 * levels
    sun_row = first_wind + 2
    sea_row = first_wind + 3

    @pl.when(sec == 0)
    def _():
        received_ref[...] = jnp.zeros_like(received_ref)

    @pl.when(sec > 0)
    def _():
        barrier = pltpu.get_barrier_semaphore()

        def greet(i, carry):
            t = lax.rem(me + i, owners)
            pl.semaphore_signal(
                barrier, inc=1, device_id=(1 + t // strips, lax.rem(t, strips)), device_id_type=MESH
            )
            return carry

        lax.fori_loop(1, owners, greet, 0)
        own_copy = pltpu.make_async_copy(trac_ref.at[1], phyto_own, own_sem)
        own_copy.start()

        def channel(c, rows):
            count = rows.stop - rows.start

            def interleaved(ref, lead, group, member):
                return jnp.concatenate(
                    [
                        ref[
                            pl.ds(
                                ((lead * width + rows.start) * halves + part) * group + member,
                                count,
                                stride=halves * group,
                            ),
                            :,
                        ]
                        for part in range(halves)
                    ],
                    axis=1,
                )

            if c < first_heat:
                return interleaved(state_ref, c // levels, levels, c % levels)
            if c < first_wind:
                return interleaved(heat_ref, 0, levels, c - first_heat)
            if c < sun_row:
                return interleaved(wind_ref, 0, 2, c - first_wind)
            if c == sun_row:
                return sun_ref[rows, :]
            return sea_ref[rows, :].astype(jnp.float32)

        spans = halo_spans(levels)
        for c, (at, count) in enumerate(spans):
            halo_out[0, at : at + count, :] = channel(c, slice(width - count, width))
            halo_out[1, at : at + count, :] = channel(c, slice(0, count))

        own_copy.wait()
        for h in range(strips):
            phyto_out[h] = phyto_own[h * levels : (h + 1) * levels, :]
        pl.semaphore_wait(barrier, owners - 1)

        def edge_copy(out_ref, in_ref, ssem, rsem, side):
            return pltpu.make_async_remote_copy(
                src_ref=out_ref.at[side],
                dst_ref=in_ref.at[side],
                send_sem=ssem.at[side],
                recv_sem=rsem.at[side],
                device_id=(sec, right if side == 0 else left),
                device_id_type=MESH,
            )

        halo_copies = [
            edge_copy(halo_out, halo_in, halo_ssem, halo_rsem, side) for side in range(2)
        ]

        def phyto_copy(t, slot):
            target = lax.rem(t, strips)
            return pltpu.make_async_remote_copy(
                src_ref=phyto_out.at[target],
                dst_ref=phyto_in.at[slot],
                send_sem=phyto_ssem.at[t],
                recv_sem=phyto_rsem.at[slot],
                device_id=(1 + t // strips, target),
                device_id_type=MESH,
            )

        def send_phyto(i, carry):
            phyto_copy(lax.rem(me + i, owners), me).start()
            return carry

        lax.fori_loop(1, owners, send_phyto, 0)
        alone = sec < 2
        takes = [alone | (lax.rem(sec, 2) == side) for side in range(2)]
        for copy, mine in zip(halo_copies, takes):
            pl.when(mine)(copy.start)

        phyto_in[me] = phyto_out[strip]

        for c in range(grid.shape[0]):
            grid[c, 0:HALO, :] = jnp.zeros((HALO, lat), jnp.float32)
            tail = width // 8 * 8 + HALO
            grid[c, tail:, :] = jnp.zeros((padded_rows - tail, lat), jnp.float32)
            grid[c, HALO : HALO + width, :] = channel(c, slice(0, width))

        def wait_phyto(i, carry):
            t = lax.rem(me + i, owners)
            phyto_copy(t, t).wait()
            return carry

        lax.fori_loop(1, owners, wait_phyto, 0)

        lat_index = lax.broadcasted_iota(jnp.int32, (lat, LANES), 0)
        lon_index = lax.broadcasted_iota(jnp.int32, (place_rows, LANES), 0)

        def spread(l, carry):
            listed = lists_ref[pl.ds(l, 1), :]
            x = listed >> lat_shift
            y = listed & (lat - 1)
            lanes = pl.ds(pl.multiple_of(l * LANES, LANES), LANES)
            onehot[:, lanes] = jnp.where(lat_index == y, 1.0, 0.0).astype(jnp.bfloat16)
            here = lon_index == x
            values = phyto_in[l]
            for k in range(levels):
                rest = values[k : k + 1, :]
                for part in range(3):
                    term = rest.astype(jnp.bfloat16).astype(jnp.float32)
                    rest = rest - term
                    row = (3 * k + part) * place_rows
                    placed[row : row + place_rows, lanes] = jnp.where(here, term, 0.0).astype(
                        jnp.bfloat16
                    )
            return carry

        lax.fori_loop(0, owners, spread, 0)
        spread_out = lax.dot_general(
            placed[...],
            onehot[...],
            (((1,), (1,)), ((), ())),
            preferred_element_type=jnp.float32,
        )
        for k in range(levels):
            base = 3 * k * place_rows
            own = (
                spread_out[base : base + width]
                + spread_out[base + place_rows : base + place_rows + width]
                + spread_out[base + 2 * place_rows : base + 2 * place_rows + width]
            )
            phyto_grid[k] = jnp.zeros((padded_rows, lat), jnp.float32)
            phyto_grid[k, HALO : HALO + width, :] = own
            rim_out[0, 2 * k : 2 * k + 2, :] = own[width - 2 : width]
            rim_out[1, 2 * k : 2 * k + 2, :] = own[0:2]

        rim_copies = [edge_copy(rim_out, rim_in, rim_ssem, rim_rsem, side) for side in range(2)]
        for copy in rim_copies:
            copy.start()
        for copy, mine in zip(halo_copies, takes):
            pl.when(mine)(copy.wait)

        @pl.when(jnp.logical_not(alone))
        def _():
            side = lax.rem(sec, 2)
            hand_on = pltpu.make_async_remote_copy(
                src_ref=halo_in.at[side],
                dst_ref=halo_in.at[side],
                send_sem=pass_ssem,
                recv_sem=pass_rsem,
                device_id=(sec + 1 - 2 * side, strip),
                device_id_type=MESH,
            )
            hand_on.start()
            hand_on.wait()

        for c, (at, count) in enumerate(spans):
            grid[c, HALO - count : HALO, :] = halo_in[0, at : at + count, :]
            grid[c, HALO + width : HALO + width + count, :] = halo_in[1, at : at + count, :]

        lane = lax.broadcasted_iota(jnp.int32, (padded_rows, lat), 1)
        not_last = lane < lat - 1
        not_first = lane > 0
        coriolis_y = CORIOLIS * (2.0 * (lane.astype(jnp.float32) + 0.5) / lat - 1.0)

        def around(field):
            east = pltpu.roll(field, padded_rows - 1, 0)
            west = pltpu.roll(field, 1, 0)
            north = jnp.where(not_last, pltpu.roll(field, lat - 1, 1), 0.0)
            south = jnp.where(not_first, pltpu.roll(field, 1, 1), 0.0)
            return east, west, north, south

        def rates(u, v, q, r, heating, k):
            def flow(field):
                east, west, north, south = around(field)
                return east + west + north + south - 4.0 * field

            def carried(field):
                east, west, north, south = around(field)
                return (
                    DIFFUSIVITY * (east + west + north + south - 4.0 * field)
                    - (u * (0.5 * (east - west)) + v * (0.5 * (north - south)))
                )

            sea = grid[sea_row]
            du = coriolis_y * v - DAMPING * u + VISCOSITY * flow(u)
            dv = -coriolis_y * u - DAMPING * v + VISCOSITY * flow(v)
            if k == 0:
                du = du + grid[first_wind]
                dv = dv + grid[first_wind + 1]
            dq = carried(q) + HEAT_GAIN * heating
            dr = carried(r)
            return [sea * d for d in (du, dv, dq, dr)]

        def ocean_step():
            for k in range(levels):
                start = [grid[f * levels + k] for f in range(4)]
                heating = grid[first_heat + k]
                first = [s + DT_OCEAN * d for s, d in zip(start, rates(*start, heating, k))]
                second = [
                    0.75 * s + 0.25 * (f + DT_OCEAN * d)
                    for s, f, d in zip(start, first, rates(*first, heating, k))
                ]
                third = [
                    ONE_THIRD * s + TWO_THIRDS * (f + DT_OCEAN * d)
                    for s, f, d in zip(start, second, rates(*second, heating, k))
                ]
                for f in range(4):
                    grid[f * levels + k] = third[f]

        def column_fields():
            total = None
            for k in range(levels - 1, 0, -1):
                u, v = grid[k], grid[levels + k]
                east = pltpu.roll(u, padded_rows - 1, 0)
                west = pltpu.roll(u, 1, 0)
                north = jnp.where(not_last, pltpu.roll(v, lat - 1, 1), 0.0)
                south = jnp.where(not_first, pltpu.roll(v, 1, 1), 0.0)
                div = 0.5 * (east - west) + 0.5 * (north - south)
                total = div if total is None else total + div
                fields[k - 1] = W_LIMIT * jnp.tanh(W_GAIN * total)
                shear = (u - grid[k - 1]) ** 2 + (v - grid[levels + k - 1]) ** 2
                fields[levels - 1 + k - 1] = KV_BASE + KV_SHEAR * shear / (1.0 + shear)

        fields[2 * (levels - 1)] = (
            grid[first_wind] * grid[first_wind] + grid[first_wind + 1] * grid[first_wind + 1]
        )

        def sent_channels():
            refs = [(grid, 2 * levels + i) for i in range(2 * levels)]
            refs += [(fields, i) for i in range(2 * levels - 1)]
            refs += [(grid, sun_row)]
            return refs

        tile_count = ceil_to(width, 8) // 8
        sublane = lax.broadcasted_iota(jnp.int32, (8, LANES), 0)

        def field_copy(step, h, slot):
            return pltpu.make_async_remote_copy(
                src_ref=send.at[step, h],
                dst_ref=recv.at[
                    step, pl.ds(pl.multiple_of(slot * ROWS_SENT, ROWS_SENT), ROWS_SENT)
                ],
                send_sem=field_ssem.at[step, h],
                recv_sem=field_rsem.at[step, slot],
                device_id=(sec, h),
                device_id_type=MESH,
            )

        def pick(step, h):
            listed = lists_ref[pl.ds((sec - 1) * strips + h, 1), :]
            x = jnp.broadcast_to(listed >> lat_shift, (8, LANES))
            y = jnp.broadcast_to(listed & (lat - 1), (8, LANES))
            low = y & (LANES - 1)
            half = y >> (LANES.bit_length() - 1)
            for c, (ref, row) in enumerate(sent_channels()):
                total = jnp.zeros((8, LANES), jnp.float32)
                for tile in range(tile_count):
                    rows = slice(HALO + 8 * tile, HALO + 8 * tile + 8)
                    for part in range(halves):
                        taken = jnp.take_along_axis(
                            ref[row, rows, part * LANES : (part + 1) * LANES],
                            low,
                            axis=1,
                            mode="promise_in_bounds",
                        )
                        mine = (x == sublane + 8 * tile) & (half == part)
                        total = jnp.where(mine, taken, total)
                send[step, h, c : c + 1, :] = jnp.sum(total, axis=0, keepdims=True)

        def send_fields(step):
            def one(i, carry):
                h = lax.rem(strip + i, strips)
                pick(step, h)
                field_copy(step, h, strip).start()
                return carry

            lax.fori_loop(1, strips, one, 0)
            pick(step, strip)
            recv[step, pl.ds(pl.multiple_of(strip * ROWS_SENT, ROWS_SENT), ROWS_SENT), :] = send[
                step, strip
            ]

        def wait_fields(step):
            def one(i, carry):
                h = lax.rem(strip + i, strips)
                field_copy(step, h, h).wait()
                return carry

            lax.fori_loop(1, strips, one, 0)

        for step in range(STEPS):
            ocean_step()
            column_fields()
            send_fields(step)
            if step == 0:
                for copy in rim_copies:
                    copy.wait()
                for k in range(levels):
                    phyto_grid[k, HALO - 2 : HALO, :] = rim_in[0, 2 * k : 2 * k + 2, :]
                    phyto_grid[k, HALO + width : HALO + width + 2, :] = rim_in[
                        1, 2 * k : 2 * k + 2, :
                    ]
                weights = transport_weights([None] + [fields[k] for k in range(levels - 1)])
                mixing = [None] + [fields[levels - 1 + k] for k in range(levels - 1)]
                moved = transport([phyto_grid[k] for k in range(levels)], weights, mixing)
                _, heats = light_profile(moved, grid[sun_row])
                for k in range(levels):
                    grid[first_heat + k] = heats[k]
        for step in range(STEPS):
            wait_fields(step)
            received_ref[step] = recv[step]


def tracer_kernel(strips, levels, recv, trac_ref, out_c, out_h):
    species = trac_ref.shape[0]
    sec = lax.axis_index("sec")

    @pl.when(sec == 0)
    def _():
        out_c[...] = trac_ref[...]
        out_h[...] = jnp.zeros_like(out_h)

    @pl.when(sec > 0)
    def _():
        def advance(step, source, last):
            def received(c):
                return recv[step, pl.ds(c, strips, stride=ROWS_SENT), :]

            def level_rows(k):
                return pl.ds(k, strips, stride=levels)

            heat_now = [received(k) for k in range(levels)]
            salt_top = received(levels)
            base = 2 * levels
            weights = transport_weights(
                [None] + [received(base + k) for k in range(levels - 1)]
            )
            mixing = [None] + [received(base + levels - 1 + k) for k in range(levels - 1)]
            power = received(base + 2 * (levels - 1))
            sunlight = received(ROWS_SENT - 1)
            valid = sunlight > 0.5
            transfer = GAS_RATE * power / (1.0 + power)

            before = [[source[n, level_rows(k), :] for k in range(levels)] for n in range(4)]
            moved = [transport(column, weights, mixing) for column in before]
            mids, heats = light_profile(moved[1], sunlight)
            surplus = []
            for k in range(levels):
                n_, p_, z_, d_ = (moved[i][k] for i in range(4))
                warm = jnp.exp(HEATUP_PER_STEP * heat_now[k])
                growth = (
                    GROWTH * warm * mids[k] / (mids[k] + 1.0) * jnp.abs(n_) / (jnp.abs(n_) + 1.0) * p_
                )
                grazing = GRAZING * warm * p_ * p_ / (p_ * p_ + 1.0) * z_
                remineral = REMINERAL * warm * d_
                changes = (
                    -growth + remineral + EXCRETION * z_,
                    growth - grazing - PHYTO_LOSS * p_,
                    ASSIMILATE * grazing - EXCRETION * z_ - ZOO_LOSS * z_,
                    (1.0 - ASSIMILATE) * grazing + PHYTO_LOSS * p_ + ZOO_LOSS * z_ - remineral,
                )
                for i in range(4):
                    out_c[i, level_rows(k), :] = jnp.where(
                        valid, moved[i][k] + DT_BIO * changes[i], before[i][k]
                    )
                surplus.append(remineral - growth)
                if last:
                    out_h[level_rows(k), :] = jnp.where(valid, heats[k], 0.0)
            for n in range(4, species):
                column = [source[n, level_rows(k), :] for k in range(levels)]
                now = transport(column, weights, mixing)
                if GAS_ON[n]:
                    limit = (
                        float(SOLUBILITY_BASE[n])
                        + float(SOLUBILITY_HEAT[n]) * heat_now[0]
                        + float(SOLUBILITY_BRINE[n]) * salt_top
                    )
                    now[0] = now[0] + DT_BIO * transfer * (limit - now[0])
                for k in range(levels):
                    change = float(YIELDS[n]) * surplus[k] - float(DECAYS[n]) * now[k]
                    out_c[n, level_rows(k), :] = jnp.where(valid, now[k] + DT_BIO * change, column[k])

        for step in range(STEPS):
            advance(step, trac_ref if step == 0 else out_c, step == STEPS - 1)


def halo_spans(levels):
    counts = [7] * (2 * levels) + [6] * (2 * levels) + [5] * levels + [6, 6, 2, 6]
    starts = np.cumsum([0] + counts)
    return [(int(at), count) for at, count in zip(starts, counts)]


def per_device(ocean_state, heat_first, wind_stress, shortwave, sea_mask, owner_cols, tracers):
    sections = lax.axis_size("sec")
    strips = lax.axis_size("gx")
    fields_count, levels, width, lat = ocean_state.shape
    owners = (sections - 1) * strips
    species = tracers.shape[0]
    padded_rows = ceil_to(width + 2 * HALO, 8)
    place_rows = ceil_to(width, 16)
    channels = 5 * levels + 4
    halves = lat // LANES
    f32 = jnp.float32
    vmem = pl.BlockSpec(memory_space=pltpu.VMEM)
    halo_rows = ceil_to(sum(halo_spans(levels)[-1]), 8)
    tracer_view = (
        tracers.reshape(species, levels, strips, LANES)
        .transpose(0, 2, 1, 3)
        .reshape(species, strips * levels, LANES)
    )
    received = pl.pallas_call(
        functools.partial(ocean_kernel, sections, strips, levels, width, lat),
        out_shape=jax.ShapeDtypeStruct((STEPS, strips * ROWS_SENT, LANES), f32),
        in_specs=[vmem] * 6 + [pl.BlockSpec(memory_space=pl.ANY)],
        out_specs=vmem,
        scratch_shapes=[
            pltpu.VMEM((channels, padded_rows, lat), f32),
            pltpu.VMEM((2, halo_rows, lat), f32),
            pltpu.VMEM((2, halo_rows, lat), f32),
            pltpu.VMEM((strips * levels, LANES), f32),
            pltpu.VMEM((strips, levels, LANES), f32),
            pltpu.VMEM((owners, levels, LANES), f32),
            pltpu.VMEM((3 * levels * place_rows, owners * LANES), jnp.bfloat16),
            pltpu.VMEM((lat, owners * LANES), jnp.bfloat16),
            pltpu.VMEM((levels, padded_rows, lat), f32),
            pltpu.VMEM((2, 2 * levels, lat), f32),
            pltpu.VMEM((2, 2 * levels, lat), f32),
            pltpu.VMEM((2 * levels - 1, padded_rows, lat), f32),
            pltpu.VMEM((STEPS, strips, ROWS_SENT, LANES), f32),
            pltpu.VMEM((STEPS, strips * ROWS_SENT, LANES), f32),
            pltpu.SemaphoreType.DMA,
            pltpu.SemaphoreType.DMA((2,)),
            pltpu.SemaphoreType.DMA((2,)),
            pltpu.SemaphoreType.DMA,
            pltpu.SemaphoreType.DMA,
            pltpu.SemaphoreType.DMA((owners,)),
            pltpu.SemaphoreType.DMA((owners,)),
            pltpu.SemaphoreType.DMA((2,)),
            pltpu.SemaphoreType.DMA((2,)),
            pltpu.SemaphoreType.DMA((STEPS, strips)),
            pltpu.SemaphoreType.DMA((STEPS, strips)),
        ],
        compiler_params=pltpu.CompilerParams(
            collective_id=0,
            has_side_effects=True,
            vmem_limit_bytes=(16 if owners * width < 512 else 56) << 20,
        ),
    )(
        ocean_state.reshape(fields_count, levels, width, halves, LANES)
        .transpose(0, 2, 3, 1, 4)
        .reshape(-1, LANES),
        heat_first.reshape(levels, width, halves, LANES).transpose(1, 2, 0, 3).reshape(-1, LANES),
        wind_stress.reshape(2, width, halves, LANES).transpose(1, 2, 0, 3).reshape(-1, LANES),
        shortwave,
        sea_mask,
        owner_cols.reshape(owners, LANES),
        tracer_view,
    )
    new_c, new_h = pl.pallas_call(
        functools.partial(tracer_kernel, strips, levels),
        out_shape=(
            jax.ShapeDtypeStruct((species, strips * levels, LANES), f32),
            jax.ShapeDtypeStruct((strips * levels, LANES), f32),
        ),
        in_specs=[vmem] * 2,
        out_specs=(vmem, vmem),
        compiler_params=pltpu.CompilerParams(vmem_limit_bytes=16 << 20),
    )(received, tracer_view)
    new_c = new_c.reshape(species, strips, levels, LANES).transpose(0, 2, 1, 3)
    new_h = new_h.reshape(strips, levels, LANES).transpose(1, 0, 2)
    return new_c.reshape(tracers.shape), new_h.reshape(levels, -1)


def solution(mesh):
    return jax.shard_map(
        per_device,
        mesh=mesh,
        in_specs=(
            P(None, None, "gx", None),
            P(None, "gx", None),
            P(None, "gx", None),
            P("gx", None),
            P("gx", None),
            P("gx", None, None, None),
            P(None, None, ("sec", "gx")),
        ),
        out_specs=(P(None, None, ("sec", "gx")), P(None, ("sec", "gx"))),
        check_vma=False,
    )
```

```python
import functools

import jax
import jax.numpy as jnp
import numpy as np
from jax import lax
from jax.experimental import pallas as pl
from jax.experimental.pallas import tpu as pltpu
from jax.sharding import PartitionSpec as P

STEPS = 2


DT_OCEAN = 0.15
VISCOSITY = 0.2
DIFFUSIVITY = 0.15
DAMPING = 0.05
CORIOLIS = 0.8
HEAT_GAIN = 4.0
ONE_THIRD = 1.0 / 3.0
TWO_THIRDS = 2.0 / 3.0
DT_BIO = 0.8
W_LIMIT = 0.35
W_GAIN = 0.25
KV_BASE = 0.05
KV_SHEAR = 0.3
GAS_RATE = 0.5
WATER_ATTEN = 0.15
CHLORO_ATTEN = 0.1
HEATUP_PER_STEP = 0.5
GROWTH = 0.6
GRAZING = 0.4
REMINERAL = 0.2
EXCRETION = 0.1
PHYTO_LOSS = 0.05
ZOO_LOSS = 0.05
ASSIMILATE = 0.6
YIELDS = np.array(
    [
        0.0,
        0.0,
        0.0,
        0.0,
        -1.3,
        1.0,
        0.16,
        0.9,
        -0.6,
        0.4,
        1.2,
        -0.8,
        0.5,
        0.3,
        -0.4,
        0.7,
        -1.0,
        0.2,
        0.6,
    ],
    np.float32,
)
DECAYS = np.array(
    [
        0.0,
        0.0,
        0.0,
        0.0,
        0.02,
        0.01,
        0.05,
        0.03,
        0.08,
        0.04,
        0.02,
        0.06,
        0.1,
        0.03,
        0.07,
        0.05,
        0.02,
        0.09,
        0.04,
    ],
    np.float32,
)
GAS_ON = np.array([0, 0, 0, 0, 1, 1] + [0] * 13, np.float32)
SOLUBILITY_BASE = np.array([0, 0, 0, 0, 1.2, 1.0] + [0] * 13, np.float32)
SOLUBILITY_HEAT = np.array([0, 0, 0, 0, -0.5, -0.3] + [0] * 13, np.float32)
SOLUBILITY_BRINE = np.array([0, 0, 0, 0, 0.1, 0.3] + [0] * 13, np.float32)

MESH = pl.DeviceIdType.MESH
HALO = 8
LANES = 128
ROWS_SENT = 16


def minmod(one_side, other_side):
    return jnp.maximum(0.0, jnp.minimum(one_side, other_side)) + jnp.minimum(
        0.0, jnp.maximum(one_side, other_side)
    )


def transport_weights(upwelling):
    return [
        None
        if w is None
        else (jnp.maximum(w, 0.0), jnp.minimum(w, 0.0), 0.5 * (1.0 - DT_BIO * jnp.abs(w)))
        for w in upwelling
    ]


def transport(column, weights, mixing):
    levels = len(column)
    diffs = [column[k + 1] - column[k] for k in range(levels - 1)]
    slopes = [None] + [minmod(diffs[k], diffs[k - 1]) for k in range(1, levels - 1)] + [None]
    flux = [None] * (levels + 1)
    for k in range(1, levels):
        up, down, half = weights[k]
        from_below = column[k] if slopes[k] is None else column[k] - half * slopes[k]
        from_above = column[k - 1] if slopes[k - 1] is None else column[k - 1] + half * slopes[k - 1]
        flux[k] = up * from_below + down * from_above + mixing[k] * diffs[k - 1]
    out = []
    for k in range(levels):
        if k == 0:
            gain = flux[1]
        elif k == levels - 1:
            gain = -flux[k]
        else:
            gain = flux[k + 1] - flux[k]
        out.append(column[k] + DT_BIO * gain)
    return out


def light_profile(phyto, sunlight):
    mids, heats = [], []
    top = sunlight
    for p in phyto:
        extinction = WATER_ATTEN + CHLORO_ATTEN * jnp.abs(p)
        mid_pass = jnp.exp(-0.5 * extinction)
        mids.append(top * mid_pass)
        after = top * jnp.exp(-extinction)
        heats.append(top - after)
        top = after
    return mids, heats


def ceil_to(value, unit):
    return (value + unit - 1) // unit * unit


def ocean_kernel(
    sections,
    strips,
    levels,
    width,
    lat,
    state_ref,
    heat_ref,
    wind_ref,
    sun_ref,
    sea_ref,
    lists_ref,
    trac_ref,
    received_ref,
    grid,
    halo_out,
    halo_in,
    phyto_own,
    phyto_out,
    phyto_in,
    placed,
    onehot,
    phyto_grid,
    rim_out,
    rim_in,
    fields,
    send,
    recv,
    own_sem,
    halo_ssem,
    halo_rsem,
    pass_ssem,
    pass_rsem,
    phyto_ssem,
    phyto_rsem,
    rim_ssem,
    rim_rsem,
    field_ssem,
    field_rsem,
):
    owners = (sections - 1) * strips
    padded_rows = grid.shape[1]
    sec = lax.axis_index("sec")
    strip = lax.axis_index("gx")
    right = lax.rem(strip + 1, strips)
    left = lax.rem(strip + strips - 1, strips)
    me = (sec - 1) * strips + strip
    lat_shift = lat.bit_length() - 1
    halves = lat // LANES
    place_rows = placed.shape[0] // (3 * levels)
    first_heat = 4 * levels
    first_wind = 5 * levels
    sun_row = first_wind + 2
    sea_row = first_wind + 3

    @pl.when(sec == 0)
    def _():
        received_ref[...] = jnp.zeros_like(received_ref)

    @pl.when(sec > 0)
    def _():
        barrier = pltpu.get_barrier_semaphore()

        def greet(i, carry):
            t = lax.rem(me + i, owners)
            pl.semaphore_signal(
                barrier, inc=1, device_id=(1 + t // strips, lax.rem(t, strips)), device_id_type=MESH
            )
            return carry

        lax.fori_loop(1, owners, greet, 0)
        own_copy = pltpu.make_async_copy(trac_ref.at[1], phyto_own, own_sem)
        own_copy.start()

        def channel(c, rows):
            count = rows.stop - rows.start

            def interleaved(ref, lead, group, member):
                return jnp.concatenate(
                    [
                        ref[
                            pl.ds(
                                ((lead * width + rows.start) * halves + part) * group + member,
                                count,
                                stride=halves * group,
                            ),
                            :,
                        ]
                        for part in range(halves)
                    ],
                    axis=1,
                )

            if c < first_heat:
                return interleaved(state_ref, c // levels, levels, c % levels)
            if c < first_wind:
                return interleaved(heat_ref, 0, levels, c - first_heat)
            if c < sun_row:
                return interleaved(wind_ref, 0, 2, c - first_wind)
            if c == sun_row:
                return sun_ref[rows, :]
            return sea_ref[rows, :].astype(jnp.float32)

        spans = halo_spans(levels)
        for c, (at, count) in enumerate(spans):
            halo_out[0, at : at + count, :] = channel(c, slice(width - count, width))
            halo_out[1, at : at + count, :] = channel(c, slice(0, count))

        own_copy.wait()
        for h in range(strips):
            phyto_out[h] = phyto_own[h * levels : (h + 1) * levels, :]
        pl.semaphore_wait(barrier, owners - 1)

        def edge_copy(out_ref, in_ref, ssem, rsem, side):
            return pltpu.make_async_remote_copy(
                src_ref=out_ref.at[side],
                dst_ref=in_ref.at[side],
                send_sem=ssem.at[side],
                recv_sem=rsem.at[side],
                device_id=(sec, right if side == 0 else left),
                device_id_type=MESH,
            )

        halo_copies = [
            edge_copy(halo_out, halo_in, halo_ssem, halo_rsem, side) for side in range(2)
        ]

        def phyto_copy(t, slot):
            target = lax.rem(t, strips)
            return pltpu.make_async_remote_copy(
                src_ref=phyto_out.at[target],
                dst_ref=phyto_in.at[slot],
                send_sem=phyto_ssem.at[t],
                recv_sem=phyto_rsem.at[slot],
                device_id=(1 + t // strips, target),
                device_id_type=MESH,
            )

        def send_phyto(i, carry):
            phyto_copy(lax.rem(me + i, owners), me).start()
            return carry

        lax.fori_loop(1, owners, send_phyto, 0)
        alone = sec < 2
        takes = [alone | (lax.rem(sec, 2) == side) for side in range(2)]
        for copy, mine in zip(halo_copies, takes):
            pl.when(mine)(copy.start)

        phyto_in[me] = phyto_out[strip]

        for c in range(grid.shape[0]):
            grid[c, 0:HALO, :] = jnp.zeros((HALO, lat), jnp.float32)
            tail = width // 8 * 8 + HALO
            grid[c, tail:, :] = jnp.zeros((padded_rows - tail, lat), jnp.float32)
            grid[c, HALO : HALO + width, :] = channel(c, slice(0, width))

        def wait_phyto(i, carry):
            t = lax.rem(me + i, owners)
            phyto_copy(t, t).wait()
            return carry

        lax.fori_loop(1, owners, wait_phyto, 0)

        lat_index = lax.broadcasted_iota(jnp.int32, (lat, LANES), 0)
        lon_index = lax.broadcasted_iota(jnp.int32, (place_rows, LANES), 0)

        def spread(l, carry):
            listed = lists_ref[pl.ds(l, 1), :]
            x = listed >> lat_shift
            y = listed & (lat - 1)
            lanes = pl.ds(pl.multiple_of(l * LANES, LANES), LANES)
            onehot[:, lanes] = jnp.where(lat_index == y, 1.0, 0.0).astype(jnp.bfloat16)
            here = lon_index == x
            values = phyto_in[l]
            for k in range(levels):
                rest = values[k : k + 1, :]
                for part in range(3):
                    term = rest.astype(jnp.bfloat16).astype(jnp.float32)
                    rest = rest - term
                    row = (3 * k + part) * place_rows
                    placed[row : row + place_rows, lanes] = jnp.where(here, term, 0.0).astype(
                        jnp.bfloat16
                    )
            return carry

        lax.fori_loop(0, owners, spread, 0)
        spread_out = lax.dot_general(
            placed[...],
            onehot[...],
            (((1,), (1,)), ((), ())),
            preferred_element_type=jnp.float32,
        )
        for k in range(levels):
            base = 3 * k * place_rows
            own = (
                spread_out[base : base + width]
                + spread_out[base + place_rows : base + place_rows + width]
                + spread_out[base + 2 * place_rows : base + 2 * place_rows + width]
            )
            phyto_grid[k] = jnp.zeros((padded_rows, lat), jnp.float32)
            phyto_grid[k, HALO : HALO + width, :] = own
            rim_out[0, 2 * k : 2 * k + 2, :] = own[width - 2 : width]
            rim_out[1, 2 * k : 2 * k + 2, :] = own[0:2]

        rim_copies = [edge_copy(rim_out, rim_in, rim_ssem, rim_rsem, side) for side in range(2)]
        for copy in rim_copies:
            copy.start()
        for copy, mine in zip(halo_copies, takes):
            pl.when(mine)(copy.wait)

        @pl.when(jnp.logical_not(alone))
        def _():
            side = lax.rem(sec, 2)
            hand_on = pltpu.make_async_remote_copy(
                src_ref=halo_in.at[side],
                dst_ref=halo_in.at[side],
                send_sem=pass_ssem,
                recv_sem=pass_rsem,
                device_id=(sec + 1 - 2 * side, strip),
                device_id_type=MESH,
            )
            hand_on.start()
            hand_on.wait()

        for c, (at, count) in enumerate(spans):
            grid[c, HALO - count : HALO, :] = halo_in[0, at : at + count, :]
            grid[c, HALO + width : HALO + width + count, :] = halo_in[1, at : at + count, :]

        lane = lax.broadcasted_iota(jnp.int32, (padded_rows, lat), 1)
        not_last = lane < lat - 1
        not_first = lane > 0
        coriolis_y = CORIOLIS * (2.0 * (lane.astype(jnp.float32) + 0.5) / lat - 1.0)

        def around(field):
            east = pltpu.roll(field, padded_rows - 1, 0)
            west = pltpu.roll(field, 1, 0)
            north = jnp.where(not_last, pltpu.roll(field, lat - 1, 1), 0.0)
            south = jnp.where(not_first, pltpu.roll(field, 1, 1), 0.0)
            return east, west, north, south

        def rates(u, v, q, r, heating, k):
            def flow(field):
                east, west, north, south = around(field)
                return east + west + north + south - 4.0 * field

            def carried(field):
                east, west, north, south = around(field)
                return (
                    DIFFUSIVITY * (east + west + north + south - 4.0 * field)
                    - (u * (0.5 * (east - west)) + v * (0.5 * (north - south)))
                )

            sea = grid[sea_row]
            du = coriolis_y * v - DAMPING * u + VISCOSITY * flow(u)
            dv = -coriolis_y * u - DAMPING * v + VISCOSITY * flow(v)
            if k == 0:
                du = du + grid[first_wind]
                dv = dv + grid[first_wind + 1]
            dq = carried(q) + HEAT_GAIN * heating
            dr = carried(r)
            return [sea * d for d in (du, dv, dq, dr)]

        def ocean_step():
            for k in range(levels):
                start = [grid[f * levels + k] for f in range(4)]
                heating = grid[first_heat + k]
                first = [s + DT_OCEAN * d for s, d in zip(start, rates(*start, heating, k))]
                second = [
                    0.75 * s + 0.25 * (f + DT_OCEAN * d)
                    for s, f, d in zip(start, first, rates(*first, heating, k))
                ]
                third = [
                    ONE_THIRD * s + TWO_THIRDS * (f + DT_OCEAN * d)
                    for s, f, d in zip(start, second, rates(*second, heating, k))
                ]
                for f in range(4):
                    grid[f * levels + k] = third[f]

        def column_fields():
            total = None
            for k in range(levels - 1, 0, -1):
                u, v = grid[k], grid[levels + k]
                east = pltpu.roll(u, padded_rows - 1, 0)
                west = pltpu.roll(u, 1, 0)
                north = jnp.where(not_last, pltpu.roll(v, lat - 1, 1), 0.0)
                south = jnp.where(not_first, pltpu.roll(v, 1, 1), 0.0)
                div = 0.5 * (east - west) + 0.5 * (north - south)
                total = div if total is None else total + div
                fields[k - 1] = W_LIMIT * jnp.tanh(W_GAIN * total)
                shear = (u - grid[k - 1]) ** 2 + (v - grid[levels + k - 1]) ** 2
                fields[levels - 1 + k - 1] = KV_BASE + KV_SHEAR * shear / (1.0 + shear)

        fields[2 * (levels - 1)] = (
            grid[first_wind] * grid[first_wind] + grid[first_wind + 1] * grid[first_wind + 1]
        )

        def sent_channels():
            refs = [(grid, 2 * levels + i) for i in range(2 * levels)]
            refs += [(fields, i) for i in range(2 * levels - 1)]
            refs += [(grid, sun_row)]
            return refs

        tile_count = ceil_to(width, 8) // 8
        sublane = lax.broadcasted_iota(jnp.int32, (8, LANES), 0)

        def field_copy(step, h, slot):
            return pltpu.make_async_remote_copy(
                src_ref=send.at[step, h],
                dst_ref=recv.at[
                    step, pl.ds(pl.multiple_of(slot * ROWS_SENT, ROWS_SENT), ROWS_SENT)
                ],
                send_sem=field_ssem.at[step, h],
                recv_sem=field_rsem.at[step, slot],
                device_id=(sec, h),
                device_id_type=MESH,
            )

        def pick(step, h):
            listed = lists_ref[pl.ds((sec - 1) * strips + h, 1), :]
            x = jnp.broadcast_to(listed >> lat_shift, (8, LANES))
            y = jnp.broadcast_to(listed & (lat - 1), (8, LANES))
            low = y & (LANES - 1)
            half = y >> (LANES.bit_length() - 1)
            for c, (ref, row) in enumerate(sent_channels()):
                total = jnp.zeros((8, LANES), jnp.float32)
                for tile in range(tile_count):
                    rows = slice(HALO + 8 * tile, HALO + 8 * tile + 8)
                    for part in range(halves):
                        taken = jnp.take_along_axis(
                            ref[row, rows, part * LANES : (part + 1) * LANES],
                            low,
                            axis=1,
                            mode="promise_in_bounds",
                        )
                        mine = (x == sublane + 8 * tile) & (half == part)
                        total = jnp.where(mine, taken, total)
                send[step, h, c : c + 1, :] = jnp.sum(total, axis=0, keepdims=True)

        def send_fields(step):
            def one(i, carry):
                h = lax.rem(strip + i, strips)
                pick(step, h)
                field_copy(step, h, strip).start()
                return carry

            lax.fori_loop(1, strips, one, 0)
            pick(step, strip)
            recv[step, pl.ds(pl.multiple_of(strip * ROWS_SENT, ROWS_SENT), ROWS_SENT), :] = send[
                step, strip
            ]

        def wait_fields(step):
            def one(i, carry):
                h = lax.rem(strip + i, strips)
                field_copy(step, h, h).wait()
                return carry

            lax.fori_loop(1, strips, one, 0)

        for step in range(STEPS):
            ocean_step()
            column_fields()
            send_fields(step)
            if step == 0:
                for copy in rim_copies:
                    copy.wait()
                for k in range(levels):
                    phyto_grid[k, HALO - 2 : HALO, :] = rim_in[0, 2 * k : 2 * k + 2, :]
                    phyto_grid[k, HALO + width : HALO + width + 2, :] = rim_in[
                        1, 2 * k : 2 * k + 2, :
                    ]
                weights = transport_weights([None] + [fields[k] for k in range(levels - 1)])
                mixing = [None] + [fields[levels - 1 + k] for k in range(levels - 1)]
                moved = transport([phyto_grid[k] for k in range(levels)], weights, mixing)
                _, heats = light_profile(moved, grid[sun_row])
                for k in range(levels):
                    grid[first_heat + k] = heats[k]
        for step in range(STEPS):
            wait_fields(step)
            received_ref[step] = recv[step]


def tracer_kernel(strips, levels, recv, trac_ref, out_c, out_h):
    species = trac_ref.shape[0]
    sec = lax.axis_index("sec")

    @pl.when(sec == 0)
    def _():
        out_c[...] = trac_ref[...]
        out_h[...] = jnp.zeros_like(out_h)

    @pl.when(sec > 0)
    def _():
        def advance(step, source, last):
            def received(c):
                return recv[step, pl.ds(c, strips, stride=ROWS_SENT), :]

            def level_rows(k):
                return pl.ds(k, strips, stride=levels)

            heat_now = [received(k) for k in range(levels)]
            salt_top = received(levels)
            base = 2 * levels
            weights = transport_weights(
                [None] + [received(base + k) for k in range(levels - 1)]
            )
            mixing = [None] + [received(base + levels - 1 + k) for k in range(levels - 1)]
            power = received(base + 2 * (levels - 1))
            sunlight = received(ROWS_SENT - 1)
            valid = sunlight > 0.5
            transfer = GAS_RATE * power / (1.0 + power)

            before = [[source[n, level_rows(k), :] for k in range(levels)] for n in range(4)]
            moved = [transport(column, weights, mixing) for column in before]
            mids, heats = light_profile(moved[1], sunlight)
            surplus = []
            for k in range(levels):
                n_, p_, z_, d_ = (moved[i][k] for i in range(4))
                warm = jnp.exp(HEATUP_PER_STEP * heat_now[k])
                growth = (
                    GROWTH * warm * mids[k] / (mids[k] + 1.0) * jnp.abs(n_) / (jnp.abs(n_) + 1.0) * p_
                )
                grazing = GRAZING * warm * p_ * p_ / (p_ * p_ + 1.0) * z_
                remineral = REMINERAL * warm * d_
                changes = (
                    -growth + remineral + EXCRETION * z_,
                    growth - grazing - PHYTO_LOSS * p_,
                    ASSIMILATE * grazing - EXCRETION * z_ - ZOO_LOSS * z_,
                    (1.0 - ASSIMILATE) * grazing + PHYTO_LOSS * p_ + ZOO_LOSS * z_ - remineral,
                )
                for i in range(4):
                    out_c[i, level_rows(k), :] = jnp.where(
                        valid, moved[i][k] + DT_BIO * changes[i], before[i][k]
                    )
                surplus.append(remineral - growth)
                if last:
                    out_h[level_rows(k), :] = jnp.where(valid, heats[k], 0.0)
            for n in range(4, species):
                column = [source[n, level_rows(k), :] for k in range(levels)]
                now = transport(column, weights, mixing)
                if GAS_ON[n]:
                    limit = (
                        float(SOLUBILITY_BASE[n])
                        + float(SOLUBILITY_HEAT[n]) * heat_now[0]
                        + float(SOLUBILITY_BRINE[n]) * salt_top
                    )
                    now[0] = now[0] + DT_BIO * transfer * (limit - now[0])
                for k in range(levels):
                    change = float(YIELDS[n]) * surplus[k] - float(DECAYS[n]) * now[k]
                    out_c[n, level_rows(k), :] = jnp.where(valid, now[k] + DT_BIO * change, column[k])

        for step in range(STEPS):
            advance(step, trac_ref if step == 0 else out_c, step == STEPS - 1)


def halo_spans(levels):
    counts = [7] * (2 * levels) + [6] * (2 * levels) + [5] * levels + [6, 6, 2, 6]
    starts = np.cumsum([0] + counts)
    return [(int(at), count) for at, count in zip(starts, counts)]


def per_device(ocean_state, heat_first, wind_stress, shortwave, sea_mask, owner_cols, tracers):
    sections = lax.axis_size("sec")
    strips = lax.axis_size("gx")
    fields_count, levels, width, lat = ocean_state.shape
    owners = (sections - 1) * strips
    species = tracers.shape[0]
    padded_rows = ceil_to(width + 2 * HALO, 8)
    place_rows = ceil_to(width, 16)
    channels = 5 * levels + 4
    halves = lat // LANES
    f32 = jnp.float32
    vmem = pl.BlockSpec(memory_space=pltpu.VMEM)
    halo_rows = ceil_to(sum(halo_spans(levels)[-1]), 8)
    tracer_view = (
        tracers.reshape(species, levels, strips, LANES)
        .transpose(0, 2, 1, 3)
        .reshape(species, strips * levels, LANES)
    )
    received = pl.pallas_call(
        functools.partial(ocean_kernel, sections, strips, levels, width, lat),
        out_shape=jax.ShapeDtypeStruct((STEPS, strips * ROWS_SENT, LANES), f32),
        in_specs=[vmem] * 6 + [pl.BlockSpec(memory_space=pl.ANY)],
        out_specs=vmem,
        scratch_shapes=[
            pltpu.VMEM((channels, padded_rows, lat), f32),
            pltpu.VMEM((2, halo_rows, lat), f32),
            pltpu.VMEM((2, halo_rows, lat), f32),
            pltpu.VMEM((strips * levels, LANES), f32),
            pltpu.VMEM((strips, levels, LANES), f32),
            pltpu.VMEM((owners, levels, LANES), f32),
            pltpu.VMEM((3 * levels * place_rows, owners * LANES), jnp.bfloat16),
            pltpu.VMEM((lat, owners * LANES), jnp.bfloat16),
            pltpu.VMEM((levels, padded_rows, lat), f32),
            pltpu.VMEM((2, 2 * levels, lat), f32),
            pltpu.VMEM((2, 2 * levels, lat), f32),
            pltpu.VMEM((2 * levels - 1, padded_rows, lat), f32),
            pltpu.VMEM((STEPS, strips, ROWS_SENT, LANES), f32),
            pltpu.VMEM((STEPS, strips * ROWS_SENT, LANES), f32),
            pltpu.SemaphoreType.DMA,
            pltpu.SemaphoreType.DMA((2,)),
            pltpu.SemaphoreType.DMA((2,)),
            pltpu.SemaphoreType.DMA,
            pltpu.SemaphoreType.DMA,
            pltpu.SemaphoreType.DMA((owners,)),
            pltpu.SemaphoreType.DMA((owners,)),
            pltpu.SemaphoreType.DMA((2,)),
            pltpu.SemaphoreType.DMA((2,)),
            pltpu.SemaphoreType.DMA((STEPS, strips)),
            pltpu.SemaphoreType.DMA((STEPS, strips)),
        ],
        compiler_params=pltpu.CompilerParams(
            collective_id=0,
            has_side_effects=True,
            vmem_limit_bytes=56 << 20,
        ),
    )(
        ocean_state.reshape(fields_count, levels, width, halves, LANES)
        .transpose(0, 2, 3, 1, 4)
        .reshape(-1, LANES),
        heat_first.reshape(levels, width, halves, LANES).transpose(1, 2, 0, 3).reshape(-1, LANES),
        wind_stress.reshape(2, width, halves, LANES).transpose(1, 2, 0, 3).reshape(-1, LANES),
        shortwave,
        sea_mask,
        owner_cols.reshape(owners, LANES),
        tracer_view,
    )
    new_c, new_h = pl.pallas_call(
        functools.partial(tracer_kernel, strips, levels),
        out_shape=(
            jax.ShapeDtypeStruct((species, strips * levels, LANES), f32),
            jax.ShapeDtypeStruct((strips * levels, LANES), f32),
        ),
        in_specs=[vmem] * 2,
        out_specs=(vmem, vmem),
        compiler_params=pltpu.CompilerParams(vmem_limit_bytes=16 << 20),
    )(received, tracer_view)
    new_c = new_c.reshape(species, strips, levels, LANES).transpose(0, 2, 1, 3)
    new_h = new_h.reshape(strips, levels, LANES).transpose(1, 0, 2)
    return new_c.reshape(tracers.shape), new_h.reshape(levels, -1)


def solution(mesh):
    return jax.shard_map(
        per_device,
        mesh=mesh,
        in_specs=(
            P(None, None, "gx", None),
            P(None, "gx", None),
            P(None, "gx", None),
            P("gx", None),
            P("gx", None),
            P("gx", None, None, None),
            P(None, None, ("sec", "gx")),
        ),
        out_specs=(P(None, None, ("sec", "gx")), P(None, ("sec", "gx"))),
        check_vma=False,
    )
```

```python
import functools

import jax
import jax.numpy as jnp
import numpy as np
from jax import lax
from jax.experimental import pallas as pl
from jax.experimental.pallas import tpu as pltpu
from jax.sharding import PartitionSpec as P

STEPS = 2


DT_OCEAN = 0.15
VISCOSITY = 0.2
DIFFUSIVITY = 0.15
DAMPING = 0.05
CORIOLIS = 0.8
HEAT_GAIN = 4.0
ONE_THIRD = 1.0 / 3.0
TWO_THIRDS = 2.0 / 3.0
DT_BIO = 0.8
W_LIMIT = 0.35
W_GAIN = 0.25
KV_BASE = 0.05
KV_SHEAR = 0.3
GAS_RATE = 0.5
WATER_ATTEN = 0.15
CHLORO_ATTEN = 0.1
HEATUP_PER_STEP = 0.5
GROWTH = 0.6
GRAZING = 0.4
REMINERAL = 0.2
EXCRETION = 0.1
PHYTO_LOSS = 0.05
ZOO_LOSS = 0.05
ASSIMILATE = 0.6
YIELDS = np.array(
    [
        0.0,
        0.0,
        0.0,
        0.0,
        -1.3,
        1.0,
        0.16,
        0.9,
        -0.6,
        0.4,
        1.2,
        -0.8,
        0.5,
        0.3,
        -0.4,
        0.7,
        -1.0,
        0.2,
        0.6,
    ],
    np.float32,
)
DECAYS = np.array(
    [
        0.0,
        0.0,
        0.0,
        0.0,
        0.02,
        0.01,
        0.05,
        0.03,
        0.08,
        0.04,
        0.02,
        0.06,
        0.1,
        0.03,
        0.07,
        0.05,
        0.02,
        0.09,
        0.04,
    ],
    np.float32,
)
GAS_ON = np.array([0, 0, 0, 0, 1, 1] + [0] * 13, np.float32)
SOLUBILITY_BASE = np.array([0, 0, 0, 0, 1.2, 1.0] + [0] * 13, np.float32)
SOLUBILITY_HEAT = np.array([0, 0, 0, 0, -0.5, -0.3] + [0] * 13, np.float32)
SOLUBILITY_BRINE = np.array([0, 0, 0, 0, 0.1, 0.3] + [0] * 13, np.float32)

MESH = pl.DeviceIdType.MESH
HALO = 8
LANES = 128
ROWS_SENT = 16


def minmod(one_side, other_side):
    return jnp.maximum(0.0, jnp.minimum(one_side, other_side)) + jnp.minimum(
        0.0, jnp.maximum(one_side, other_side)
    )


def transport_weights(upwelling):
    return [
        None
        if w is None
        else (jnp.maximum(w, 0.0), jnp.minimum(w, 0.0), 0.5 * (1.0 - DT_BIO * jnp.abs(w)))
        for w in upwelling
    ]


def transport(column, weights, mixing):
    levels = len(column)
    diffs = [column[k + 1] - column[k] for k in range(levels - 1)]
    slopes = [None] + [minmod(diffs[k], diffs[k - 1]) for k in range(1, levels - 1)] + [None]
    flux = [None] * (levels + 1)
    for k in range(1, levels):
        up, down, half = weights[k]
        from_below = column[k] if slopes[k] is None else column[k] - half * slopes[k]
        from_above = column[k - 1] if slopes[k - 1] is None else column[k - 1] + half * slopes[k - 1]
        flux[k] = up * from_below + down * from_above + mixing[k] * diffs[k - 1]
    out = []
    for k in range(levels):
        if k == 0:
            gain = flux[1]
        elif k == levels - 1:
            gain = -flux[k]
        else:
            gain = flux[k + 1] - flux[k]
        out.append(column[k] + DT_BIO * gain)
    return out


def light_profile(phyto, sunlight):
    mids, heats = [], []
    top = sunlight
    for p in phyto:
        extinction = WATER_ATTEN + CHLORO_ATTEN * jnp.abs(p)
        mid_pass = jnp.exp(-0.5 * extinction)
        mids.append(top * mid_pass)
        after = top * jnp.exp(-extinction)
        heats.append(top - after)
        top = after
    return mids, heats


def ceil_to(value, unit):
    return (value + unit - 1) // unit * unit


def ocean_kernel(
    sections,
    strips,
    levels,
    width,
    lat,
    state_ref,
    heat_ref,
    wind_ref,
    sun_ref,
    sea_ref,
    lists_ref,
    trac_ref,
    received_ref,
    grid,
    halo_out,
    halo_in,
    phyto_own,
    phyto_out,
    phyto_in,
    placed,
    onehot,
    phyto_grid,
    rim_out,
    rim_in,
    fields,
    send,
    recv,
    own_sem,
    halo_ssem,
    halo_rsem,
    pass_ssem,
    pass_rsem,
    phyto_ssem,
    phyto_rsem,
    rim_ssem,
    rim_rsem,
    field_ssem,
    field_rsem,
):
    owners = (sections - 1) * strips
    padded_rows = grid.shape[1]
    sec = lax.axis_index("sec")
    strip = lax.axis_index("gx")
    right = lax.rem(strip + 1, strips)
    left = lax.rem(strip + strips - 1, strips)
    me = (sec - 1) * strips + strip
    lat_shift = lat.bit_length() - 1
    halves = lat // LANES
    place_rows = placed.shape[0] // (3 * levels)
    first_heat = 4 * levels
    first_wind = 5 * levels
    sun_row = first_wind + 2
    sea_row = first_wind + 3

    @pl.when(sec == 0)
    def _():
        received_ref[...] = jnp.zeros_like(received_ref)

    @pl.when(sec > 0)
    def _():
        barrier = pltpu.get_barrier_semaphore()

        def greet(i, carry):
            t = lax.rem(me + i, owners)
            pl.semaphore_signal(
                barrier, inc=1, device_id=(1 + t // strips, lax.rem(t, strips)), device_id_type=MESH
            )
            return carry

        lax.fori_loop(1, owners, greet, 0)
        own_copy = pltpu.make_async_copy(trac_ref.at[1], phyto_own, own_sem)
        own_copy.start()

        def channel(c, rows):
            count = rows.stop - rows.start

            def interleaved(ref, lead, group, member):
                return jnp.concatenate(
                    [
                        ref[
                            pl.ds(
                                ((lead * width + rows.start) * halves + part) * group + member,
                                count,
                                stride=halves * group,
                            ),
                            :,
                        ]
                        for part in range(halves)
                    ],
                    axis=1,
                )

            if c < first_heat:
                return interleaved(state_ref, c // levels, levels, c % levels)
            if c < first_wind:
                return interleaved(heat_ref, 0, levels, c - first_heat)
            if c < sun_row:
                return interleaved(wind_ref, 0, 2, c - first_wind)
            if c == sun_row:
                return sun_ref[rows, :]
            return sea_ref[rows, :].astype(jnp.float32)

        spans = halo_spans(levels)
        for c, (at, count) in enumerate(spans):
            halo_out[0, at : at + count, :] = channel(c, slice(width - count, width))
            halo_out[1, at : at + count, :] = channel(c, slice(0, count))

        own_copy.wait()
        for h in range(strips):
            phyto_out[h] = phyto_own[h * levels : (h + 1) * levels, :]
        pl.semaphore_wait(barrier, owners - 1)

        def edge_copy(out_ref, in_ref, ssem, rsem, side):
            return pltpu.make_async_remote_copy(
                src_ref=out_ref.at[side],
                dst_ref=in_ref.at[side],
                send_sem=ssem.at[side],
                recv_sem=rsem.at[side],
                device_id=(sec, right if side == 0 else left),
                device_id_type=MESH,
            )

        halo_copies = [
            edge_copy(halo_out, halo_in, halo_ssem, halo_rsem, side) for side in range(2)
        ]

        def phyto_copy(t, slot):
            target = lax.rem(t, strips)
            return pltpu.make_async_remote_copy(
                src_ref=phyto_out.at[target],
                dst_ref=phyto_in.at[slot],
                send_sem=phyto_ssem.at[t],
                recv_sem=phyto_rsem.at[slot],
                device_id=(1 + t // strips, target),
                device_id_type=MESH,
            )

        def send_phyto(i, carry):
            phyto_copy(lax.rem(me + i, owners), me).start()
            return carry

        alone = sec < 2
        takes = [alone | (lax.rem(sec, 2) == side) for side in range(2)]
        for copy, mine in zip(halo_copies, takes):
            pl.when(mine)(copy.start)

        lax.fori_loop(1, owners, send_phyto, 0)

        phyto_in[me] = phyto_out[strip]

        for c in range(grid.shape[0]):
            grid[c, 0:HALO, :] = jnp.zeros((HALO, lat), jnp.float32)
            tail = width // 8 * 8 + HALO
            grid[c, tail:, :] = jnp.zeros((padded_rows - tail, lat), jnp.float32)
            grid[c, HALO : HALO + width, :] = channel(c, slice(0, width))

        def wait_phyto(i, carry):
            t = lax.rem(me + i, owners)
            phyto_copy(t, t).wait()
            return carry

        lax.fori_loop(1, owners, wait_phyto, 0)

        lat_index = lax.broadcasted_iota(jnp.int32, (lat, LANES), 0)
        lon_index = lax.broadcasted_iota(jnp.int32, (place_rows, LANES), 0)

        def spread(l, carry):
            listed = lists_ref[pl.ds(l, 1), :]
            x = listed >> lat_shift
            y = listed & (lat - 1)
            lanes = pl.ds(pl.multiple_of(l * LANES, LANES), LANES)
            onehot[:, lanes] = jnp.where(lat_index == y, 1.0, 0.0).astype(jnp.bfloat16)
            here = lon_index == x
            values = phyto_in[l]
            for k in range(levels):
                rest = values[k : k + 1, :]
                for part in range(3):
                    term = rest.astype(jnp.bfloat16).astype(jnp.float32)
                    rest = rest - term
                    row = (3 * k + part) * place_rows
                    placed[row : row + place_rows, lanes] = jnp.where(here, term, 0.0).astype(
                        jnp.bfloat16
                    )
            return carry

        lax.fori_loop(0, owners, spread, 0)
        spread_out = lax.dot_general(
            placed[...],
            onehot[...],
            (((1,), (1,)), ((), ())),
            preferred_element_type=jnp.float32,
        )
        for k in range(levels):
            base = 3 * k * place_rows
            own = (
                spread_out[base : base + width]
                + spread_out[base + place_rows : base + place_rows + width]
                + spread_out[base + 2 * place_rows : base + 2 * place_rows + width]
            )
            phyto_grid[k] = jnp.zeros((padded_rows, lat), jnp.float32)
            phyto_grid[k, HALO : HALO + width, :] = own
            rim_out[0, 2 * k : 2 * k + 2, :] = own[width - 2 : width]
            rim_out[1, 2 * k : 2 * k + 2, :] = own[0:2]

        rim_copies = [edge_copy(rim_out, rim_in, rim_ssem, rim_rsem, side) for side in range(2)]
        for copy in rim_copies:
            copy.start()
        for copy, mine in zip(halo_copies, takes):
            pl.when(mine)(copy.wait)

        @pl.when(jnp.logical_not(alone))
        def _():
            side = lax.rem(sec, 2)
            hand_on = pltpu.make_async_remote_copy(
                src_ref=halo_in.at[side],
                dst_ref=halo_in.at[side],
                send_sem=pass_ssem,
                recv_sem=pass_rsem,
                device_id=(sec + 1 - 2 * side, strip),
                device_id_type=MESH,
            )
            hand_on.start()
            hand_on.wait()

        for c, (at, count) in enumerate(spans):
            grid[c, HALO - count : HALO, :] = halo_in[0, at : at + count, :]
            grid[c, HALO + width : HALO + width + count, :] = halo_in[1, at : at + count, :]

        lane = lax.broadcasted_iota(jnp.int32, (padded_rows, lat), 1)
        not_last = lane < lat - 1
        not_first = lane > 0
        coriolis_y = CORIOLIS * (2.0 * (lane.astype(jnp.float32) + 0.5) / lat - 1.0)

        def around(field):
            east = pltpu.roll(field, padded_rows - 1, 0)
            west = pltpu.roll(field, 1, 0)
            north = jnp.where(not_last, pltpu.roll(field, lat - 1, 1), 0.0)
            south = jnp.where(not_first, pltpu.roll(field, 1, 1), 0.0)
            return east, west, north, south

        def rates(u, v, q, r, heating, k):
            def flow(field):
                east, west, north, south = around(field)
                return east + west + north + south - 4.0 * field

            def carried(field):
                east, west, north, south = around(field)
                return (
                    DIFFUSIVITY * (east + west + north + south - 4.0 * field)
                    - (u * (0.5 * (east - west)) + v * (0.5 * (north - south)))
                )

            sea = grid[sea_row]
            du = coriolis_y * v - DAMPING * u + VISCOSITY * flow(u)
            dv = -coriolis_y * u - DAMPING * v + VISCOSITY * flow(v)
            if k == 0:
                du = du + grid[first_wind]
                dv = dv + grid[first_wind + 1]
            dq = carried(q) + HEAT_GAIN * heating
            dr = carried(r)
            return [sea * d for d in (du, dv, dq, dr)]

        def ocean_step():
            for k in range(levels):
                start = [grid[f * levels + k] for f in range(4)]
                heating = grid[first_heat + k]
                first = [s + DT_OCEAN * d for s, d in zip(start, rates(*start, heating, k))]
                second = [
                    0.75 * s + 0.25 * (f + DT_OCEAN * d)
                    for s, f, d in zip(start, first, rates(*first, heating, k))
                ]
                third = [
                    ONE_THIRD * s + TWO_THIRDS * (f + DT_OCEAN * d)
                    for s, f, d in zip(start, second, rates(*second, heating, k))
                ]
                for f in range(4):
                    grid[f * levels + k] = third[f]

        def column_fields():
            total = None
            for k in range(levels - 1, 0, -1):
                u, v = grid[k], grid[levels + k]
                east = pltpu.roll(u, padded_rows - 1, 0)
                west = pltpu.roll(u, 1, 0)
                north = jnp.where(not_last, pltpu.roll(v, lat - 1, 1), 0.0)
                south = jnp.where(not_first, pltpu.roll(v, 1, 1), 0.0)
                div = 0.5 * (east - west) + 0.5 * (north - south)
                total = div if total is None else total + div
                fields[k - 1] = W_LIMIT * jnp.tanh(W_GAIN * total)
                shear = (u - grid[k - 1]) ** 2 + (v - grid[levels + k - 1]) ** 2
                fields[levels - 1 + k - 1] = KV_BASE + KV_SHEAR * shear / (1.0 + shear)

        fields[2 * (levels - 1)] = (
            grid[first_wind] * grid[first_wind] + grid[first_wind + 1] * grid[first_wind + 1]
        )

        def sent_channels():
            refs = [(grid, 2 * levels + i) for i in range(2 * levels)]
            refs += [(fields, i) for i in range(2 * levels - 1)]
            refs += [(grid, sun_row)]
            return refs

        tile_count = ceil_to(width, 8) // 8
        sublane = lax.broadcasted_iota(jnp.int32, (8, LANES), 0)

        def field_copy(step, h, slot):
            return pltpu.make_async_remote_copy(
                src_ref=send.at[step, h],
                dst_ref=recv.at[
                    step, pl.ds(pl.multiple_of(slot * ROWS_SENT, ROWS_SENT), ROWS_SENT)
                ],
                send_sem=field_ssem.at[step, h],
                recv_sem=field_rsem.at[step, slot],
                device_id=(sec, h),
                device_id_type=MESH,
            )

        def pick(step, h):
            listed = lists_ref[pl.ds((sec - 1) * strips + h, 1), :]
            x = jnp.broadcast_to(listed >> lat_shift, (8, LANES))
            y = jnp.broadcast_to(listed & (lat - 1), (8, LANES))
            low = y & (LANES - 1)
            half = y >> (LANES.bit_length() - 1)
            for c, (ref, row) in enumerate(sent_channels()):
                total = jnp.zeros((8, LANES), jnp.float32)
                for tile in range(tile_count):
                    rows = slice(HALO + 8 * tile, HALO + 8 * tile + 8)
                    for part in range(halves):
                        taken = jnp.take_along_axis(
                            ref[row, rows, part * LANES : (part + 1) * LANES],
                            low,
                            axis=1,
                            mode="promise_in_bounds",
                        )
                        mine = (x == sublane + 8 * tile) & (half == part)
                        total = jnp.where(mine, taken, total)
                send[step, h, c : c + 1, :] = jnp.sum(total, axis=0, keepdims=True)

        def send_fields(step):
            def one(i, carry):
                h = lax.rem(strip + i, strips)
                pick(step, h)
                field_copy(step, h, strip).start()
                return carry

            lax.fori_loop(1, strips, one, 0)
            pick(step, strip)
            recv[step, pl.ds(pl.multiple_of(strip * ROWS_SENT, ROWS_SENT), ROWS_SENT), :] = send[
                step, strip
            ]

        def wait_fields(step):
            def one(i, carry):
                h = lax.rem(strip + i, strips)
                field_copy(step, h, h).wait()
                return carry

            lax.fori_loop(1, strips, one, 0)

        for step in range(STEPS):
            ocean_step()
            column_fields()
            send_fields(step)
            if step == 0:
                for copy in rim_copies:
                    copy.wait()
                for k in range(levels):
                    phyto_grid[k, HALO - 2 : HALO, :] = rim_in[0, 2 * k : 2 * k + 2, :]
                    phyto_grid[k, HALO + width : HALO + width + 2, :] = rim_in[
                        1, 2 * k : 2 * k + 2, :
                    ]
                weights = transport_weights([None] + [fields[k] for k in range(levels - 1)])
                mixing = [None] + [fields[levels - 1 + k] for k in range(levels - 1)]
                moved = transport([phyto_grid[k] for k in range(levels)], weights, mixing)
                _, heats = light_profile(moved, grid[sun_row])
                for k in range(levels):
                    grid[first_heat + k] = heats[k]
        for step in range(STEPS):
            wait_fields(step)
            received_ref[step] = recv[step]


def tracer_kernel(strips, levels, recv, trac_ref, out_c, out_h):
    species = trac_ref.shape[0]
    sec = lax.axis_index("sec")

    @pl.when(sec == 0)
    def _():
        out_c[...] = trac_ref[...]
        out_h[...] = jnp.zeros_like(out_h)

    @pl.when(sec > 0)
    def _():
        def advance(step, source, last):
            def received(c):
                return recv[step, pl.ds(c, strips, stride=ROWS_SENT), :]

            def level_rows(k):
                return pl.ds(k, strips, stride=levels)

            heat_now = [received(k) for k in range(levels)]
            salt_top = received(levels)
            base = 2 * levels
            weights = transport_weights(
                [None] + [received(base + k) for k in range(levels - 1)]
            )
            mixing = [None] + [received(base + levels - 1 + k) for k in range(levels - 1)]
            power = received(base + 2 * (levels - 1))
            sunlight = received(ROWS_SENT - 1)
            valid = sunlight > 0.5
            transfer = GAS_RATE * power / (1.0 + power)

            before = [[source[n, level_rows(k), :] for k in range(levels)] for n in range(4)]
            moved = [transport(column, weights, mixing) for column in before]
            mids, heats = light_profile(moved[1], sunlight)
            surplus = []
            for k in range(levels):
                n_, p_, z_, d_ = (moved[i][k] for i in range(4))
                warm = jnp.exp(HEATUP_PER_STEP * heat_now[k])
                growth = (
                    GROWTH * warm * mids[k] / (mids[k] + 1.0) * jnp.abs(n_) / (jnp.abs(n_) + 1.0) * p_
                )
                grazing = GRAZING * warm * p_ * p_ / (p_ * p_ + 1.0) * z_
                remineral = REMINERAL * warm * d_
                changes = (
                    -growth + remineral + EXCRETION * z_,
                    growth - grazing - PHYTO_LOSS * p_,
                    ASSIMILATE * grazing - EXCRETION * z_ - ZOO_LOSS * z_,
                    (1.0 - ASSIMILATE) * grazing + PHYTO_LOSS * p_ + ZOO_LOSS * z_ - remineral,
                )
                for i in range(4):
                    out_c[i, level_rows(k), :] = jnp.where(
                        valid, moved[i][k] + DT_BIO * changes[i], before[i][k]
                    )
                surplus.append(remineral - growth)
                if last:
                    out_h[level_rows(k), :] = jnp.where(valid, heats[k], 0.0)
            for n in range(4, species):
                column = [source[n, level_rows(k), :] for k in range(levels)]
                now = transport(column, weights, mixing)
                if GAS_ON[n]:
                    limit = (
                        float(SOLUBILITY_BASE[n])
                        + float(SOLUBILITY_HEAT[n]) * heat_now[0]
                        + float(SOLUBILITY_BRINE[n]) * salt_top
                    )
                    now[0] = now[0] + DT_BIO * transfer * (limit - now[0])
                for k in range(levels):
                    change = float(YIELDS[n]) * surplus[k] - float(DECAYS[n]) * now[k]
                    out_c[n, level_rows(k), :] = jnp.where(valid, now[k] + DT_BIO * change, column[k])

        for step in range(STEPS):
            advance(step, trac_ref if step == 0 else out_c, step == STEPS - 1)


def halo_spans(levels):
    counts = [7] * (2 * levels) + [6] * (2 * levels) + [5] * levels + [6, 6, 2, 6]
    starts = np.cumsum([0] + counts)
    return [(int(at), count) for at, count in zip(starts, counts)]


def per_device(ocean_state, heat_first, wind_stress, shortwave, sea_mask, owner_cols, tracers):
    sections = lax.axis_size("sec")
    strips = lax.axis_size("gx")
    fields_count, levels, width, lat = ocean_state.shape
    owners = (sections - 1) * strips
    species = tracers.shape[0]
    padded_rows = ceil_to(width + 2 * HALO, 8)
    place_rows = ceil_to(width, 16)
    channels = 5 * levels + 4
    halves = lat // LANES
    f32 = jnp.float32
    vmem = pl.BlockSpec(memory_space=pltpu.VMEM)
    halo_rows = ceil_to(sum(halo_spans(levels)[-1]), 8)
    tracer_view = (
        tracers.reshape(species, levels, strips, LANES)
        .transpose(0, 2, 1, 3)
        .reshape(species, strips * levels, LANES)
    )
    received = pl.pallas_call(
        functools.partial(ocean_kernel, sections, strips, levels, width, lat),
        out_shape=jax.ShapeDtypeStruct((STEPS, strips * ROWS_SENT, LANES), f32),
        in_specs=[vmem] * 6 + [pl.BlockSpec(memory_space=pl.ANY)],
        out_specs=vmem,
        scratch_shapes=[
            pltpu.VMEM((channels, padded_rows, lat), f32),
            pltpu.VMEM((2, halo_rows, lat), f32),
            pltpu.VMEM((2, halo_rows, lat), f32),
            pltpu.VMEM((strips * levels, LANES), f32),
            pltpu.VMEM((strips, levels, LANES), f32),
            pltpu.VMEM((owners, levels, LANES), f32),
            pltpu.VMEM((3 * levels * place_rows, owners * LANES), jnp.bfloat16),
            pltpu.VMEM((lat, owners * LANES), jnp.bfloat16),
            pltpu.VMEM((levels, padded_rows, lat), f32),
            pltpu.VMEM((2, 2 * levels, lat), f32),
            pltpu.VMEM((2, 2 * levels, lat), f32),
            pltpu.VMEM((2 * levels - 1, padded_rows, lat), f32),
            pltpu.VMEM((STEPS, strips, ROWS_SENT, LANES), f32),
            pltpu.VMEM((STEPS, strips * ROWS_SENT, LANES), f32),
            pltpu.SemaphoreType.DMA,
            pltpu.SemaphoreType.DMA((2,)),
            pltpu.SemaphoreType.DMA((2,)),
            pltpu.SemaphoreType.DMA,
            pltpu.SemaphoreType.DMA,
            pltpu.SemaphoreType.DMA((owners,)),
            pltpu.SemaphoreType.DMA((owners,)),
            pltpu.SemaphoreType.DMA((2,)),
            pltpu.SemaphoreType.DMA((2,)),
            pltpu.SemaphoreType.DMA((STEPS, strips)),
            pltpu.SemaphoreType.DMA((STEPS, strips)),
        ],
        compiler_params=pltpu.CompilerParams(
            collective_id=0,
            has_side_effects=True,
            vmem_limit_bytes=56 << 20,
        ),
    )(
        ocean_state.reshape(fields_count, levels, width, halves, LANES)
        .transpose(0, 2, 3, 1, 4)
        .reshape(-1, LANES),
        heat_first.reshape(levels, width, halves, LANES).transpose(1, 2, 0, 3).reshape(-1, LANES),
        wind_stress.reshape(2, width, halves, LANES).transpose(1, 2, 0, 3).reshape(-1, LANES),
        shortwave,
        sea_mask,
        owner_cols.reshape(owners, LANES),
        tracer_view,
    )
    new_c, new_h = pl.pallas_call(
        functools.partial(tracer_kernel, strips, levels),
        out_shape=(
            jax.ShapeDtypeStruct((species, strips * levels, LANES), f32),
            jax.ShapeDtypeStruct((strips * levels, LANES), f32),
        ),
        in_specs=[vmem] * 2,
        out_specs=(vmem, vmem),
        compiler_params=pltpu.CompilerParams(vmem_limit_bytes=16 << 20),
    )(received, tracer_view)
    new_c = new_c.reshape(species, strips, levels, LANES).transpose(0, 2, 1, 3)
    new_h = new_h.reshape(strips, levels, LANES).transpose(1, 0, 2)
    return new_c.reshape(tracers.shape), new_h.reshape(levels, -1)


def solution(mesh):
    return jax.shard_map(
        per_device,
        mesh=mesh,
        in_specs=(
            P(None, None, "gx", None),
            P(None, "gx", None),
            P(None, "gx", None),
            P("gx", None),
            P("gx", None),
            P("gx", None, None, None),
            P(None, None, ("sec", "gx")),
        ),
        out_specs=(P(None, None, ("sec", "gx")), P(None, ("sec", "gx"))),
        check_vma=False,
    )
```
